256 devices in a mesh: hid: 128 (over x, z, y), seq: 2 (over core).
Axes of the slice: x: 4, y: 4, z: 8, core: 2. Of those that a mesh axis runs over, the one named last changes fastest.
Arguments:
- pre_act: bfloat16 [1536, 32768], P(('hid', 'seq')), may hold values from -6 to 6
- butterfly: bfloat16 [128, 5, 256, 256], P('hid'), may hold values from -0.15625 to 0.15625
- low_u: bfloat16 [32768, 256], P('hid'), may hold values from -0.25 to 0.25
- low_v: bfloat16 [256, 32768], P(None, 'hid'), may hold values from -0.0625 to 0.0625
- grad_out: bfloat16 [1536, 32768], P(('hid', 'seq')), may hold values from -6 to 6
Outputs:
- output: bfloat16 [1536, 32768], P(('hid', 'seq'))
- grad_pre: bfloat16 [1536, 32768], P(('hid', 'seq'))
- grad_butterfly: float32 [128, 5, 256, 256], P('hid', None, 'seq')
- grad_low_u: float32 [32768, 256], P('hid', 'seq')
- grad_low_v: float32 [256, 32768], P('seq', 'hid')
The draws below stay inside these ranges and needn't reach their ends.
All inputs are finite; a program needn't handle non-finite values.
Results may differ from the reference program's by a relative error of at most 0.0075.
Values may be sent and summed in bfloat16 or wider, within the bound.
A program may use at most 64 MiB of HBM per device.

```python
import math
import jax
import jax.numpy as jnp
import numpy as np

B = 256
LEVELS = 4
R = 256
FF = 32768
BLOCKS = 128
TOKENS = 1536


def block_levels(rng, shape, shards, least, top_value):
    loudness, own = 1.0, jax.random.fold_in(rng, 6)
    for axis_at, shards_of in shards:
        heights = jnp.exp(jax.random.uniform(jax.random.fold_in(own, axis_at), (shards_of,), jnp.float32, least / len(shards), top_value / len(shards)))
        loudness = loudness * jnp.repeat(heights, shape[axis_at] // shards_of).reshape([-1 if axis == axis_at else 1 for axis in range(len(shape))])
    return loudness


def noise(stream_key, extent, deviation, most, shards=(), dtype=jnp.bfloat16):
    array = deviation * jax.random.normal(stream_key, extent, jnp.float32)
    if shards:
        array = array * block_levels(stream_key, extent, shards, -0.22, 0.18)
    return jnp.clip(array, -most, most).astype(dtype)


def setup_inputs(seed: int = 0) -> dict:
    arg_keys = jax.random.split(jax.random.key(seed), 6)
    return {
        "pre_act": noise(arg_keys[0], (TOKENS, FF), 1.0, 6.0, ((0, 256),)),
        "butterfly": noise(arg_keys[1], (BLOCKS, LEVELS + 1, B, B), ((LEVELS + 1) * B) ** -0.5, 0.15625, ((0, 128),)),
        "low_u": noise(arg_keys[2], (FF, R), (FF // 64) ** -0.5, 0.25, ((0, 128),)),
        "low_v": noise(arg_keys[3], (R, FF), (FF // 4) ** -0.5, 0.0625, ((1, 128),)),
        "grad_out": noise(arg_keys[4], (TOKENS, FF), 1.0, 6.0, ((0, 256),)),
    }


def gelu_tanh(value):
    return jax.nn.gelu(value, approximate=True)

def reference(pre_act, butterfly, low_u, low_v, grad_out):
    pre_f = pre_act.astype(jnp.float32)
    act = gelu_tanh(pre_f).astype(jnp.bfloat16)
    latent = jnp.dot(act, low_u, preferred_element_type=jnp.float32).astype(jnp.bfloat16)
    act_blocks = act.reshape(TOKENS, BLOCKS, B)
    grad_blocks = grad_out.reshape(TOKENS, BLOCKS, B)
    grad_float = grad_blocks.astype(jnp.float32)
    order = np.arange(BLOCKS)
    total = jnp.dot(latent, low_v, preferred_element_type=jnp.float32).reshape(TOKENS, BLOCKS, B)
    backward = jnp.zeros((TOKENS, BLOCKS, B), jnp.float32)
    weight_grads = []
    for level in range(LEVELS + 1):
        source = order if level == 0 else order ^ 1 << level - 1
        moved = act_blocks[:, source, :].astype(jnp.float32)
        weights = butterfly[:, level].astype(jnp.float32)
        total = total + jnp.einsum('tjb,jbc->tjc', moved, weights)
        grad_moved = grad_float[:, source, :]
        weights_moved = butterfly[source, level].astype(jnp.float32)
        backward = backward + jnp.einsum('tic,ibc->tib', grad_moved, weights_moved)
        weight_grads.append(jnp.einsum('tjb,tjc->jbc', moved, grad_float))
    output = total.reshape(TOKENS, FF).astype(jnp.bfloat16)
    dlatent = jnp.dot(grad_out, low_v.T, preferred_element_type=jnp.float32).astype(jnp.bfloat16)
    backward = backward.reshape(TOKENS, FF) + jnp.dot(dlatent, low_u.T, preferred_element_type=jnp.float32)
    grad_act = backward.astype(jnp.bfloat16)
    unused, pullback = jax.vjp(gelu_tanh, pre_f)
    grad_pre = pullback(grad_act.astype(jnp.float32))[0].astype(jnp.bfloat16)
    factor = 1.0 / math.sqrt(TOKENS)
    grad_butterfly = jnp.stack(weight_grads, axis=1) * factor
    grad_low_u = jnp.dot(act.T, dlatent, preferred_element_type=jnp.float32) * factor
    grad_low_v = jnp.dot(latent.T, grad_out, preferred_element_type=jnp.float32) * factor
    return (output, grad_pre, grad_butterfly, grad_low_u, grad_low_v)
```

```python
import math

import jax
import jax.numpy as jnp
from jax import lax
from jax.sharding import PartitionSpec as P

LEVELS = 4


def swapped(x, axis, stride):
    return lax.ppermute(x, axis, [(i, i ^ 1 << stride) for i in range(lax.axis_size(axis))])


def gelu_tanh(value):
    return jax.nn.gelu(value, approximate=True)


def reduce_latents(first, second):
    both = jnp.concatenate([first, second], axis=1)
    rows, wide = both.shape
    flat = both.reshape(rows * wide // 128, 128)
    part = lax.psum_scatter(flat, "hid", scatter_dimension=0, tiled=True)
    full = lax.all_gather(part.astype(jnp.bfloat16), "hid", axis=0, tiled=True)
    full = full.reshape(rows, wide)
    return full[:, : wide // 2], full[:, wide // 2 :]


def inner_rows(left, right):
    return lax.dot_general(
        left, right, (((0,), (0,)), ((), ())), preferred_element_type=jnp.float32
    )


def on_device(pre_act, butterfly, low_u, low_v, grad_out):
    pre_f = pre_act.astype(jnp.float32)
    act_tok = gelu_tanh(pre_f).astype(jnp.bfloat16)
    act_rows = lax.all_to_all(act_tok, "hid", split_axis=1, concat_axis=0, tiled=True)
    partners = [act_rows]
    for level in range(LEVELS):
        partners.append(swapped(act_rows, "hid", level))
    grad_rows = lax.all_to_all(grad_out, "hid", split_axis=1, concat_axis=0, tiled=True)
    latent, dlatent = reduce_latents(
        jnp.dot(act_rows, low_u, preferred_element_type=jnp.float32),
        jnp.dot(grad_rows, low_v.T, preferred_element_type=jnp.float32),
    )
    total = jnp.dot(latent, low_v, preferred_element_type=jnp.float32)
    for level in range(LEVELS + 1):
        total = total + jnp.dot(
            partners[level], butterfly[0, level], preferred_element_type=jnp.float32
        )
    output_rows = total.astype(jnp.bfloat16)
    output_tok = lax.all_to_all(output_rows, "hid", split_axis=0, concat_axis=1, tiled=True)
    backward = jnp.dot(dlatent, low_u.T, preferred_element_type=jnp.float32)
    backward = backward + jnp.dot(grad_rows, butterfly[0, 0].T, preferred_element_type=jnp.float32)
    for level in range(1, LEVELS + 1):
        grad_far, weight_far = swapped((grad_rows, butterfly[0, level]), "hid", level - 1)
        backward = backward + jnp.dot(grad_far, weight_far.T, preferred_element_type=jnp.float32)
    grad_act = backward.astype(jnp.bfloat16)
    tokens_all = pre_act.shape[0] * lax.axis_size("hid") * lax.axis_size("seq")
    factor = 1.0 / math.sqrt(tokens_all)
    block_grads = jnp.stack(
        [inner_rows(partners[level], grad_rows) for level in range(LEVELS + 1)], axis=0
    )
    block_grads = block_grads[None] * factor
    low_u_grad = inner_rows(act_rows, dlatent) * factor
    low_v_grad = inner_rows(latent, grad_rows) * factor
    grad_butterfly, grad_low_u, grad_low_v = (
        lax.psum_scatter(
            block_grads.astype(jnp.bfloat16), "seq", scatter_dimension=2, tiled=True
        ).astype(jnp.float32),
        lax.psum_scatter(
            low_u_grad.astype(jnp.bfloat16), "seq", scatter_dimension=1, tiled=True
        ).astype(jnp.float32),
        lax.psum_scatter(
            low_v_grad.astype(jnp.bfloat16), "seq", scatter_dimension=0, tiled=True
        ).astype(jnp.float32),
    )
    grad_act_tok = lax.all_to_all(grad_act, "hid", split_axis=0, concat_axis=1, tiled=True)
    unused, pullback = jax.vjp(gelu_tanh, pre_f)
    grad_pre = pullback(grad_act_tok.astype(jnp.float32))[0].astype(jnp.bfloat16)
    return (output_tok, grad_pre, grad_butterfly, grad_low_u, grad_low_v)


def solution(mesh):
    in_specs = (
        P(("hid", "seq"), None),
        P("hid", None, None, None),
        P("hid", None),
        P(None, "hid"),
        P(("hid", "seq"), None),
    )
    out_specs = (
        P(("hid", "seq"), None),
        P(("hid", "seq"), None),
        P("hid", None, "seq", None),
        P("hid", "seq"),
        P("seq", "hid"),
    )
    return jax.shard_map(
        on_device, mesh=mesh, in_specs=in_specs, out_specs=out_specs, check_vma=False
    )
```

```python
import functools
import math

import jax
import jax.numpy as jnp
from jax import lax
from jax.experimental import pallas as pl
from jax.experimental.pallas import tpu as pltpu
from jax.sharding import Mesh
from jax.sharding import PartitionSpec as P

MESH = pl.DeviceIdType.MESH
BF, F32 = jnp.bfloat16, jnp.float32
GROUPS = 32
FACTOR = 1.0 / math.sqrt(1536)


def flip(value, bit):
    step = 1 << bit
    return value + step - 2 * step * lax.rem(lax.div(value, step), 2)


def dot(a, b):
    return jnp.dot(a, b, preferred_element_type=F32)


def dot_t(a, b):
    return lax.dot_general(a, b, (((1,), (1,)), ((), ())), preferred_element_type=F32)


def t_dot(a, b):
    return lax.dot_general(a, b, (((0,), (0,)), ((), ())), preferred_element_type=F32)


def cols(start, size, unit):
    return pl.ds(pl.multiple_of(start, unit), size)


def kernel(
    act, grad, bfly, low_u, low_v,
    out_tok, gact_tok, wg_out,
    A, G, G1, G2, W, acc_o, acc_g, stage, lat_send, lat_recv, lat_own, lat_all,
    wg_send, wg_recv, send_sem, recv_sem,
):
    x, z, y, c = (lax.axis_index(n) for n in ("x", "z", "y", "seq"))
    me = x * 8 + z
    sib = 1 - c
    mine, other = cols(c * 128, 128, 128), cols(sib * 128, 128, 128)
    z1, z2 = flip(z, 0), flip(z, 1)

    def remote(src, dst, ch, **dev):
        pltpu.make_async_remote_copy(
            src_ref=src, dst_ref=dst, send_sem=send_sem.at[ch], recv_sem=recv_sem.at[ch],
            device_id=dev, device_id_type=MESH,
        ).start()

    def local(src, dst, ch):
        pltpu.make_async_copy(src, dst, recv_sem.at[ch]).start()

    def arrived(ref, ch):
        pltpu.make_async_copy(ref, ref, recv_sem.at[ch]).wait()

    def sent(ref, ch):
        pltpu.make_async_copy(ref, ref, send_sem.at[ch]).wait()

    def peer(d):
        q = lax.rem(me + d, GROUPS)
        return q, lax.div(q, 8), lax.rem(q, 8)

    def ypeer(d):
        return lax.rem(y + d, 4)

    barrier = pltpu.get_barrier_semaphore()

    @pl.loop(1, GROUPS)
    def _(d):
        q, qx, qz = peer(d)
        pl.semaphore_signal(barrier, 1, device_id={"x": qx, "z": qz}, device_id_type=MESH)

    for d in range(1, 4):
        pl.semaphore_signal(barrier, 1, device_id={"y": ypeer(d)}, device_id_type=MESH)
    pl.semaphore_signal(barrier, 1, device_id={"seq": sib}, device_id_type=MESH)
    pl.semaphore_wait(barrier, GROUPS + 3)

    def scatter(src, dst, ch):
        @pl.loop(1, GROUPS)
        def _(d):
            q, qx, qz = peer(d)
            remote(src.at[q], dst.at[me], ch, x=qx, z=qz)

        local(src.at[me], dst.at[me], ch)

    scatter(grad, G.at[c], 0)
    local(bfly, W.at[y, pl.ds(0, 5)], 1)
    local(low_u, W.at[y, 5], 1)
    local(low_v, W.at[y, 6], 1)
    remote(bfly.at[3, mine], W.at[y, 7, mine], 2, z=z1)
    remote(bfly.at[4, mine], W.at[y, 8, mine], 3, z=z2)
    for d in range(1, 4):
        remote(low_u.at[mine], W.at[y, 5, mine], 3 + d, y=ypeer(d))
        remote(low_v.at[mine], W.at[y, 6, mine], 3 + d, y=ypeer(d))
        remote(bfly.at[:, mine], W.at[y, pl.ds(0, 5), mine], 3 + d, y=ypeer(d))
    scatter(act, A.at[0, c], 7)

    arrived(W.at[y, 7, mine], 2)
    arrived(W.at[y, 8, mine], 3)
    far = pl.ds(7, 2)
    for d in range(1, 4):
        remote(W.at[y, far, mine], W.at[y, far, mine], 7 + d, y=ypeer(d))
    remote(W.at[y, far, mine], W.at[y, far, mine], 11, seq=sib)

    arrived(G.at[c], 0)
    remote(G.at[c], G1, 12, z=z1)
    remote(G.at[c], G2, 13, z=z2)
    remote(G.at[c], G.at[c], 14, seq=sib)
    arrived(A.at[0, c], 7)
    remote(A.at[0, c], A.at[1, c], 15, z=z1)
    remote(A.at[0, c], A.at[2, c], 16, z=z2)
    remote(A.at[0, c], A.at[0, c], 17, seq=sib)

    near = pl.ds(0, 7)
    for d in range(1, 4):
        ys = ypeer(4 - d)
        arrived(W.at[ys, near, mine], 3 + d)
        remote(W.at[ys, near, mine], W.at[ys, near, mine], 17 + d, seq=sib)
    arrived(W.at[y, near], 1)
    for d in range(1, 4):
        arrived(W.at[ypeer(4 - d), near, other], 17 + d)

    def block(ref, b):
        return ref[:, :, :, cols(b * 256, 256, 256)].reshape(192, 256)

    A0, G0 = A.at[0, c], G.at[c]

    lat = dlat = None
    for b in range(4):
        u = dot(block(A0, b), W[b, 5])
        v = dot_t(block(G0, b), W[b, 6])
        lat, dlat = (u, v) if b == 0 else (lat + u, dlat + v)
    lat_send[:, :, :, 0:256] = lat.astype(BF).reshape(GROUPS, 3, 2, 256)
    lat_send[:, :, :, 256:512] = dlat.astype(BF).reshape(GROUPS, 3, 2, 256)
    scatter(lat_send, lat_recv, 21)

    for d in range(1, 4):
        ys = ypeer(4 - d)
        arrived(W.at[ys, far, mine], 7 + d)
        remote(W.at[ys, far, mine], W.at[ys, far, mine], 21 + d, seq=sib)

    @pl.loop(0, 4)
    def _(b):
        b1, b2 = flip(b, 0), flip(b, 1)
        here = cols(b * 256, 256, 256)
        acc_o[:, here] = (
            dot(block(A0, b), W[b, 0]) + dot(block(A0, b1), W[b, 1]) + dot(block(A0, b2), W[b, 2])
        )
        acc_g[:, here] = (
            dot_t(block(G0, b), W[b, 0])
            + dot_t(block(G0, b1), W[b1, 1])
            + dot_t(block(G0, b2), W[b2, 2])
        )

    arrived(lat_recv, 21)
    total = lat_recv[0].astype(F32)
    for q in range(1, GROUPS):
        total = total + lat_recv[q].astype(F32)
    lat_own[...] = total.astype(BF)

    @pl.loop(1, GROUPS)
    def _(d):
        q, qx, qz = peer(d)
        remote(lat_own, lat_all.at[c, me], 25, x=qx, z=qz)

    local(lat_own, lat_all.at[c, me], 25)

    arrived(G1, 12)
    arrived(G2, 13)
    arrived(A.at[1, c], 15)
    remote(A.at[1, c], A.at[1, c], 26, seq=sib)
    arrived(A.at[2, c], 16)
    remote(A.at[2, c], A.at[2, c], 27, seq=sib)
    arrived(W.at[y, far, other], 11)
    for d in range(1, 4):
        arrived(W.at[ypeer(4 - d), far, other], 21 + d)
    A1, A2 = A.at[1, c], A.at[2, c]

    arrived(lat_all.at[c], 25)
    remote(lat_all.at[c], lat_all.at[c], 28, seq=sib)
    pair = lat_all[c].reshape(192, 512)

    @pl.loop(0, 4)
    def _(b):
        here = cols(b * 256, 256, 256)
        o = (
            acc_o[:, here] + dot(block(A1, b), W[b, 3]) + dot(block(A2, b), W[b, 4])
            + dot(pair[:, 0:256], W[b, 6])
        )
        stage[0, :, :, :, here] = o.astype(BF).reshape(GROUPS, 3, 2, 256)
        g = (
            acc_g[:, here] + dot_t(block(G1, b), W[b, 7]) + dot_t(block(G2, b), W[b, 8])
            + dot_t(pair[:, 256:512], W[b, 5])
        )
        stage[1, :, :, :, here] = g.astype(BF).reshape(GROUPS, 3, 2, 256)

    for which, ref in ((0, out_tok), (1, gact_tok)):
        @pl.loop(1, GROUPS)
        def _(d):
            q, qx, qz = peer(d)
            remote(stage.at[which, q], ref.at[me], 29 + which, x=qx, z=qz)

        local(stage.at[which, me], ref.at[me], 29 + which)

    arrived(G.at[sib], 14)
    arrived(A.at[0, sib], 17)
    arrived(A.at[1, sib], 26)
    arrived(A.at[2, sib], 27)
    arrived(lat_all.at[sib], 28)
    lat_half = lat_all[:, :, :, :, cols(c * 128, 128, 128)].reshape(384, 128)
    dlat_half = lat_all[:, :, :, :, cols(256 + c * 128, 128, 128)].reshape(384, 128)

    def half(level, b):
        return A[level, :, :, :, :, cols(b * 256 + c * 128, 128, 128)].reshape(384, 128)

    for d in range(4):
        b = ypeer(d)
        whole = cols(b * 256, 256, 256)
        g = G[:, :, :, :, whole].reshape(384, 256)
        a = A[0, :, :, :, :, whole].reshape(384, 256)
        sums = [
            t_dot(half(0, b), g),
            t_dot(half(0, flip(b, 0)), g),
            t_dot(half(0, flip(b, 1)), g),
            t_dot(half(1, b), g),
            t_dot(half(2, b), g),
            t_dot(dlat_half, a),
            t_dot(lat_half, g),
        ]
        for k, value in enumerate(sums):
            if d == 0:
                wg_out[k] = value * FACTOR
            else:
                wg_send[d - 1, k] = (value * FACTOR).astype(BF)
        if d:
            remote(wg_send.at[d - 1], wg_recv.at[d - 1], 30 + d, y=b)
    for d in range(1, 4):
        arrived(wg_recv.at[d - 1], 30 + d)
        for k in range(7):
            wg_out[k] = wg_out[k] + wg_recv[d - 1, k].astype(F32)
    arrived(stage.at[0], 29)
    arrived(stage.at[1], 30)

    most = pl.ds(0, GROUPS - 1)
    sent(G.at[0, most], 0)
    sent(W.at[0, 7, pl.ds(0, 128)], 2)
    sent(W.at[0, 8, pl.ds(0, 128)], 3)
    for d in range(1, 4):
        sent(W.at[0, near, pl.ds(0, 128)], 3 + d)
        sent(W.at[0, far, pl.ds(0, 128)], 7 + d)
        sent(W.at[0, near, pl.ds(0, 128)], 17 + d)
        sent(W.at[0, far, pl.ds(0, 128)], 21 + d)
        sent(wg_send.at[d - 1], 30 + d)
    sent(W.at[0, far, pl.ds(0, 128)], 11)
    sent(A.at[0, 0, most], 7)
    for ch in (12, 13, 14, 15, 16, 17, 26, 27):
        sent(G.at[0], ch)
    sent(lat_send.at[most], 21)
    sent(lat_all.at[0, most], 25)
    sent(lat_all.at[0], 28)
    sent(stage.at[0, most], 29)
    sent(stage.at[1, most], 30)


def exchange(act, grad, bfly, low_u, low_v):
    tok = (GROUPS, 3, 2, 1024)
    any_space = pl.BlockSpec(memory_space=pl.ANY)
    vmem = pl.BlockSpec(memory_space=pltpu.VMEM)
    return pl.pallas_call(
        kernel,
        out_shape=(
            jax.ShapeDtypeStruct(tok, BF),
            jax.ShapeDtypeStruct(tok, BF),
            jax.ShapeDtypeStruct((7, 128, 256), F32),
        ),
        in_specs=[any_space] * 5,
        out_specs=(any_space, any_space, vmem),
        scratch_shapes=[
            pltpu.VMEM((3, 2) + tok, BF),
            pltpu.VMEM((2,) + tok, BF),
            pltpu.VMEM(tok, BF),
            pltpu.VMEM(tok, BF),
            pltpu.VMEM((4, 9, 256, 256), BF),
            pltpu.VMEM((192, 1024), F32),
            pltpu.VMEM((192, 1024), F32),
            pltpu.VMEM((2,) + tok, BF),
            pltpu.VMEM((GROUPS, 3, 2, 512), BF),
            pltpu.VMEM((GROUPS, 3, 2, 512), BF),
            pltpu.VMEM((3, 2, 512), BF),
            pltpu.VMEM((2, GROUPS, 3, 2, 512), BF),
            pltpu.VMEM((3, 7, 128, 256), BF),
            pltpu.VMEM((3, 7, 128, 256), BF),
            pltpu.SemaphoreType.DMA((34,)),
            pltpu.SemaphoreType.DMA((34,)),
        ],
        compiler_params=pltpu.CompilerParams(
            collective_id=0, has_side_effects=True, vmem_limit_bytes=48 * 2**20
        ),
    )(act, grad, bfly, low_u, low_v)


def gelu_tanh(value):
    return jax.nn.gelu(value, approximate=True)


def by_group(rows):
    return rows.reshape(3, 2, GROUPS, 1024).transpose(2, 0, 1, 3)


def by_token(groups):
    return groups.transpose(1, 2, 0, 3).reshape(6, 32768)


def on_device(pre_act, butterfly, low_u, low_v, grad_out):
    pre_f = pre_act.astype(F32)
    act_tok = gelu_tanh(pre_f).astype(BF)
    out_g, gact_g, wg = exchange(
        by_group(act_tok), by_group(grad_out), butterfly[0], low_u, low_v
    )
    unused, pullback = jax.vjp(gelu_tanh, pre_f)
    grad_pre = pullback(by_token(gact_g).astype(F32))[0].astype(BF)
    return by_token(out_g), grad_pre, wg[None, 0:5], wg[5].T, wg[6]


def solution(mesh):
    whole = Mesh(mesh.devices.reshape(4, 8, 4, 2), ("x", "z", "y", "seq"))
    hid = ("x", "z", "y")
    tokens = P(hid + ("seq",), None)
    return jax.shard_map(
        on_device,
        mesh=whole,
        in_specs=(tokens, P(hid, None, None, None), P(hid, None), P(None, hid), tokens),
        out_specs=(tokens, tokens, P(hid, None, "seq", None), P(hid, "seq"), P("seq", hid)),
        check_vma=False,
    )
```

```python
import functools
import math

import jax
import jax.numpy as jnp
from jax import lax
from jax.experimental import pallas as pl
from jax.experimental.pallas import tpu as pltpu
from jax.sharding import Mesh
from jax.sharding import PartitionSpec as P

MESH = pl.DeviceIdType.MESH
BF, F32 = jnp.bfloat16, jnp.float32
GROUPS = 32
FACTOR = 1.0 / math.sqrt(1536)


def flip(value, bit):
    step = 1 << bit
    return value + step - 2 * step * lax.rem(lax.div(value, step), 2)


def dot(a, b):
    return jnp.dot(a, b, preferred_element_type=F32)


def dot_t(a, b):
    return lax.dot_general(a, b, (((1,), (1,)), ((), ())), preferred_element_type=F32)


def t_dot(a, b):
    return lax.dot_general(a, b, (((0,), (0,)), ((), ())), preferred_element_type=F32)


def cols(start, size, unit):
    return pl.ds(pl.multiple_of(start, unit), size)


CHANNELS = (
    "g", "a", "own", "zfar3", "zfar4", "g1", "g2", "gsib", "asib0", "asib1", "asib2", "farsib",
    "latz", "bcz", "latsib", "out", "gact", "a1h0", "a1h1", "a2h0", "a2h1",
) + tuple(
    name + str(d)
    for name in ("low", "lows", "fly", "flys", "far", "fars", "latx", "bcx", "wa", "wb", "wc")
    for d in (1, 2, 3)
)
CH = {name: i for i, name in enumerate(CHANNELS)}


def kernel(
    act, grad, bfly, low_u, low_v,
    out_tok, gact_tok, wg_out,
    A, G, DA, DG, DG1, DG2, W, acc_o, acc_g, stage, lat_send, latx_recv, latx, latz_recv,
    lat_own, lat_all, wg_send, wg_recv, send_sem, recv_sem,
):
    x, z, y, c = (lax.axis_index(n) for n in ("x", "z", "y", "seq"))
    me = x * 8 + z
    sib = 1 - c
    mine, other = cols(c * 128, 128, 128), cols(sib * 128, 128, 128)
    z1, z2 = flip(z, 0), flip(z, 1)

    def remote(src, dst, ch, **dev):
        pltpu.make_async_remote_copy(
            src_ref=src, dst_ref=dst, send_sem=send_sem.at[CH[ch]], recv_sem=recv_sem.at[CH[ch]],
            device_id=dev, device_id_type=MESH,
        ).start()

    def local(src, dst, ch):
        pltpu.make_async_copy(src, dst, recv_sem.at[CH[ch]]).start()

    def arrived(ref, ch):
        pltpu.make_async_copy(ref, ref, recv_sem.at[CH[ch]]).wait()

    def sent(ref, ch):
        pltpu.make_async_copy(ref, ref, send_sem.at[CH[ch]]).wait()

    def peer(d):
        q = lax.rem(me + d, GROUPS)
        return q, lax.div(q, 8), lax.rem(q, 8)

    def ypeer(d):
        return lax.rem(y + d, 4)

    def xpeer(d):
        return lax.rem(x + d, 4)

    def xrows(xv):
        return pl.ds(xv * 8, 8)

    barrier = pltpu.get_barrier_semaphore()

    @pl.loop(1, GROUPS)
    def _(d):
        q, qx, qz = peer(d)
        pl.semaphore_signal(barrier, 1, device_id={"x": qx, "z": qz}, device_id_type=MESH)

    for d in range(1, 4):
        pl.semaphore_signal(barrier, 1, device_id={"y": ypeer(d)}, device_id_type=MESH)
    pl.semaphore_signal(barrier, 1, device_id={"seq": sib}, device_id_type=MESH)
    pl.semaphore_wait(barrier, GROUPS + 3)

    def scatter(src, dst, ch):
        @pl.loop(1, GROUPS)
        def _(d):
            q, qx, qz = peer(d)
            remote(src.at[q], dst.at[me], ch, x=qx, z=qz)

        local(src.at[me], dst.at[me], ch)

    fly, low, far = pl.ds(0, 5), pl.ds(5, 2), pl.ds(7, 2)
    scatter(grad, G.at[0], "g")
    local(bfly, W.at[y, fly], "own")
    local(low_u, W.at[y, 5], "own")
    local(low_v, W.at[y, 6], "own")
    for d in range(1, 4):
        remote(low_u.at[mine], W.at[y, 5, mine], f"low{d}", y=ypeer(d))
        remote(low_v.at[mine], W.at[y, 6, mine], f"low{d}", y=ypeer(d))
    remote(bfly.at[3, mine], W.at[y, 7, mine], "zfar3", z=z1)
    remote(bfly.at[4, mine], W.at[y, 8, mine], "zfar4", z=z2)
    scatter(act, A.at[0], "a")
    for d in range(1, 4):
        remote(bfly.at[:, mine], W.at[y, fly, mine], f"fly{d}", y=ypeer(d))

    for d in range(1, 4):
        ys = ypeer(4 - d)
        arrived(W.at[ys, low, mine], f"low{d}")
        remote(W.at[ys, low, mine], W.at[ys, low, mine], f"lows{d}", seq=sib)

    def dense(raw, out):
        @pl.loop(0, 4)
        def _(b):
            here = cols(b * 256, 256, 256)
            out[:, here] = raw[:, :, :, here].reshape(192, 256)

    arrived(G.at[0], "g")
    remote(G.at[0], G.at[2], "g2", z=z2)
    remote(G.at[0], G.at[1], "g1", z=z1)
    dense(G.at[0], DG.at[c])
    remote(DG.at[c], DG.at[c], "gsib", seq=sib)

    arrived(W.at[y, 7, mine], "zfar3")
    arrived(W.at[y, 8, mine], "zfar4")
    for d in range(1, 4):
        remote(W.at[y, far, mine], W.at[y, far, mine], f"far{d}", y=ypeer(d))
    remote(W.at[y, far, mine], W.at[y, far, mine], "farsib", seq=sib)

    arrived(A.at[0], "a")
    dense(A.at[0], DA.at[0, c])
    remote(DA.at[0, c], DA.at[0, c], "asib0", seq=sib)
    A0, G0 = DA.at[0, c], DG.at[c]

    arrived(W.at[y, pl.ds(0, 7)], "own")
    for d in range(1, 4):
        arrived(W.at[ypeer(4 - d), low, other], f"lows{d}")
    lat = dlat = None
    for b in range(4):
        u = dot(A0[:, b * 256 : b * 256 + 256], W[b, 5])
        v = dot_t(G0[:, b * 256 : b * 256 + 256], W[b, 6])
        lat, dlat = (u, v) if b == 0 else (lat + u, dlat + v)
    lat_send[:, :, :, 0:256] = lat.astype(BF).reshape(GROUPS, 3, 2, 256)
    lat_send[:, :, :, 256:512] = dlat.astype(BF).reshape(GROUPS, 3, 2, 256)
    for d in range(1, 4):
        remote(lat_send.at[xrows(xpeer(d))], latx_recv.at[d - 1], f"latx{d}", x=xpeer(d))

    for d in range(1, 4):
        ys = ypeer(4 - d)
        arrived(W.at[ys, fly, mine], f"fly{d}")
        remote(W.at[ys, fly, mine], W.at[ys, fly, mine], f"flys{d}", seq=sib)

    total = lat_send[xrows(x)].astype(F32)
    for d in range(1, 4):
        arrived(latx_recv.at[d - 1], f"latx{d}")
        total = total + latx_recv[d - 1].astype(F32)
    latx[...] = total.astype(BF)
    for d in range(1, 8):
        zp = lax.rem(z + d, 8)
        remote(latx.at[zp], latz_recv.at[z], "latz", z=zp)
    local(latx.at[z], latz_recv.at[z], "latz")

    first, second = pl.ds(0, 16), pl.ds(16, 16)
    remote(A.at[0, first], A.at[2, first], "a2h0", z=z2)
    remote(A.at[0, first], A.at[1, first], "a1h0", z=z1)

    for d in range(1, 4):
        arrived(W.at[ypeer(4 - d), fly, other], f"flys{d}")

    @pl.loop(0, 4)
    def _(b):
        b1, b2 = flip(b, 0), flip(b, 1)
        h0, h1, h2 = (cols(v * 256, 256, 256) for v in (b, b1, b2))
        acc_o[:, h0] = dot(A0[:, h0], W[b, 0]) + dot(A0[:, h1], W[b, 1]) + dot(A0[:, h2], W[b, 2])
        acc_g[:, h0] = (
            dot_t(G0[:, h0], W[b, 0]) + dot_t(G0[:, h1], W[b1, 1]) + dot_t(G0[:, h2], W[b2, 2])
        )

    arrived(latz_recv, "latz")
    total = latz_recv[0].astype(F32)
    for q in range(1, 8):
        total = total + latz_recv[q].astype(F32)
    lat_own[...] = total.astype(BF)
    for d in range(1, 8):
        remote(lat_own, lat_all.at[c, me], "bcz", z=lax.rem(z + d, 8))
    local(lat_own, lat_all.at[c, me], "bcz")
    remote(A.at[0, second], A.at[2, second], "a2h1", z=z2)
    remote(A.at[0, second], A.at[1, second], "a1h1", z=z1)

    def half(level, b):
        return DA[level, :, :, cols(b * 256 + c * 128, 128, 128)].reshape(384, 128)

    def gblock(b):
        return DG[:, :, cols(b * 256, 256, 256)].reshape(384, 256)

    def keep(d, k, value):
        if d == 0:
            wg_out[k] = value * FACTOR
        else:
            wg_send[d - 1, k] = (value * FACTOR).astype(BF)

    def ship(d, name, rows):
        if d:
            remote(wg_send.at[d - 1, rows], wg_recv.at[d - 1, rows], f"{name}{d}", y=ypeer(d))

    part_a, part_b, part_c = pl.ds(0, 3), pl.ds(5, 2), pl.ds(3, 2)
    arrived(DG.at[sib], "gsib")
    arrived(DA.at[0, sib], "asib0")
    for d in (2, 1, 3, 0):
        b = ypeer(d)
        g = gblock(b)
        keep(d, 0, t_dot(half(0, b), g))
        keep(d, 1, t_dot(half(0, flip(b, 0)), g))
        keep(d, 2, t_dot(half(0, flip(b, 1)), g))
        ship(d, "wa", part_a)

    for d in range(1, 4):
        ys = ypeer(4 - d)
        arrived(W.at[ys, far, mine], f"far{d}")
        remote(W.at[ys, far, mine], W.at[ys, far, mine], f"fars{d}", seq=sib)

    arrived(lat_all.at[c, xrows(x)], "bcz")
    for d in range(1, 4):
        rows = xrows(x)
        remote(lat_all.at[c, rows], lat_all.at[c, rows], f"bcx{d}", x=xpeer(d))

    arrived(G.at[1], "g1")
    dense(G.at[1], DG1)
    arrived(G.at[2], "g2")
    dense(G.at[2], DG2)
    arrived(W.at[y, far, other], "farsib")
    for d in range(1, 4):
        arrived(W.at[ypeer(4 - d), far, other], f"fars{d}")
    for d in range(1, 4):
        arrived(lat_all.at[c, xrows(xpeer(4 - d))], f"bcx{d}")
    remote(lat_all.at[c], lat_all.at[c], "latsib", seq=sib)
    pair = lat_all[c].reshape(192, 512)

    @pl.loop(0, 4)
    def _(b):
        here = cols(b * 256, 256, 256)
        g = (
            acc_g[:, here] + dot_t(DG1[:, here], W[b, 7]) + dot_t(DG2[:, here], W[b, 8])
            + dot_t(pair[:, 256:512], W[b, 5])
        )
        stage[1, :, :, :, here] = g.astype(BF).reshape(GROUPS, 3, 2, 256)

    def gather(which, ref, ch):
        @pl.loop(1, GROUPS)
        def _(d):
            q, qx, qz = peer(d)
            remote(stage.at[which, q], ref.at[me], ch, x=qx, z=qz)

        local(stage.at[which, me], ref.at[me], ch)

    gather(1, gact_tok, "gact")

    arrived(lat_all.at[sib], "latsib")
    lat_half = lat_all[:, :, :, :, cols(c * 128, 128, 128)].reshape(384, 128)
    dlat_half = lat_all[:, :, :, :, cols(256 + c * 128, 128, 128)].reshape(384, 128)
    for d in (2, 1, 3, 0):
        b = ypeer(d)
        keep(d, 5, t_dot(dlat_half, DA[0, :, :, cols(b * 256, 256, 256)].reshape(384, 256)))
        keep(d, 6, t_dot(lat_half, gblock(b)))
        ship(d, "wb", part_b)

    for half_rows, n in ((first, 0), (second, 1)):
        arrived(A.at[2, half_rows], f"a2h{n}")
        arrived(A.at[1, half_rows], f"a1h{n}")
    dense(A.at[1], DA.at[1, c])
    dense(A.at[2], DA.at[2, c])
    remote(DA.at[1, c], DA.at[1, c], "asib1", seq=sib)
    remote(DA.at[2, c], DA.at[2, c], "asib2", seq=sib)
    A1, A2 = DA.at[1, c], DA.at[2, c]

    @pl.loop(0, 4)
    def _(b):
        here = cols(b * 256, 256, 256)
        o = (
            acc_o[:, here] + dot(A1[:, here], W[b, 3]) + dot(A2[:, here], W[b, 4])
            + dot(pair[:, 0:256], W[b, 6])
        )
        stage[0, :, :, :, here] = o.astype(BF).reshape(GROUPS, 3, 2, 256)

    gather(0, out_tok, "out")

    arrived(DA.at[1, sib], "asib1")
    arrived(DA.at[2, sib], "asib2")
    for d in (2, 1, 3, 0):
        b = ypeer(d)
        g = gblock(b)
        keep(d, 3, t_dot(half(1, b), g))
        keep(d, 4, t_dot(half(2, b), g))
        ship(d, "wc", part_c)

    for name, start, count in (("wa", 0, 3), ("wb", 5, 2), ("wc", 3, 2)):
        for d in range(1, 4):
            arrived(wg_recv.at[d - 1, pl.ds(start, count)], f"{name}{d}")
        for k in range(start, start + count):
            far_sum = wg_recv[0, k].astype(F32) + wg_recv[1, k].astype(F32)
            wg_out[k] = wg_out[k] + far_sum + wg_recv[2, k].astype(F32)
    arrived(stage.at[1], "gact")
    arrived(stage.at[0], "out")

    most = pl.ds(0, GROUPS - 1)
    top = pl.ds(0, 128)
    sent(G.at[0, most], "g")
    sent(A.at[0, most], "a")
    sent(W.at[0, 7, top], "zfar3")
    sent(W.at[0, 8, top], "zfar4")
    sent(W.at[0, far, top], "farsib")
    for d in range(1, 4):
        sent(W.at[0, low, top], f"low{d}")
        sent(W.at[0, low, top], f"lows{d}")
        sent(W.at[0, fly, top], f"fly{d}")
        sent(W.at[0, fly, top], f"flys{d}")
        sent(W.at[0, far, top], f"far{d}")
        sent(W.at[0, far, top], f"fars{d}")
        sent(latx, f"latx{d}")
        sent(latx, f"bcx{d}")
        sent(wg_send.at[d - 1, part_a], f"wa{d}")
        sent(wg_send.at[d - 1, part_b], f"wb{d}")
        sent(wg_send.at[d - 1, part_c], f"wc{d}")
    sent(G.at[0], "g1")
    sent(G.at[0], "g2")
    for ch in ("gsib", "asib0", "asib1", "asib2"):
        sent(DG.at[0], ch)
    for ch in ("a1h0", "a1h1", "a2h0", "a2h1"):
        sent(A.at[0, first], ch)
    sent(latx.at[pl.ds(0, 7)], "latz")
    sent(latx.at[pl.ds(0, 7)], "bcz")
    sent(lat_all.at[0], "latsib")
    sent(stage.at[0, most], "out")
    sent(stage.at[1, most], "gact")


def exchange(act, grad, bfly, low_u, low_v):
    tok = (GROUPS, 3, 2, 1024)
    any_space = pl.BlockSpec(memory_space=pl.ANY)
    vmem = pl.BlockSpec(memory_space=pltpu.VMEM)
    return pl.pallas_call(
        kernel,
        out_shape=(
            jax.ShapeDtypeStruct(tok, BF),
            jax.ShapeDtypeStruct(tok, BF),
            jax.ShapeDtypeStruct((7, 128, 256), F32),
        ),
        in_specs=[any_space] * 5,
        out_specs=(any_space, any_space, vmem),
        scratch_shapes=[
            pltpu.VMEM((3,) + tok, BF),
            pltpu.VMEM((3,) + tok, BF),
            pltpu.VMEM((3, 2, 192, 1024), BF),
            pltpu.VMEM((2, 192, 1024), BF),
            pltpu.VMEM((192, 1024), BF),
            pltpu.VMEM((192, 1024), BF),
            pltpu.VMEM((4, 9, 256, 256), BF),
            pltpu.VMEM((192, 1024), F32),
            pltpu.VMEM((192, 1024), F32),
            pltpu.VMEM((2,) + tok, BF),
            pltpu.VMEM((GROUPS, 3, 2, 512), BF),
            pltpu.VMEM((3, 8, 3, 2, 512), BF),
            pltpu.VMEM((8, 3, 2, 512), BF),
            pltpu.VMEM((8, 3, 2, 512), BF),
            pltpu.VMEM((3, 2, 512), BF),
            pltpu.VMEM((2, GROUPS, 3, 2, 512), BF),
            pltpu.VMEM((3, 7, 128, 256), BF),
            pltpu.VMEM((3, 7, 128, 256), BF),
            pltpu.SemaphoreType.DMA((len(CHANNELS),)),
            pltpu.SemaphoreType.DMA((len(CHANNELS),)),
        ],
        compiler_params=pltpu.CompilerParams(
            collective_id=0, has_side_effects=True, vmem_limit_bytes=48 * 2**20
        ),
    )(act, grad, bfly, low_u, low_v)


def gelu_tanh(value):
    return jax.nn.gelu(value, approximate=True)


def by_group(rows):
    return rows.reshape(3, 2, GROUPS, 1024).transpose(2, 0, 1, 3)


def by_token(groups):
    return groups.transpose(1, 2, 0, 3).reshape(6, 32768)


def on_device(pre_act, butterfly, low_u, low_v, grad_out):
    pre_f = pre_act.astype(F32)
    act_tok = gelu_tanh(pre_f).astype(BF)
    out_g, gact_g, wg = exchange(
        by_group(act_tok), by_group(grad_out), butterfly[0], low_u, low_v
    )
    unused, pullback = jax.vjp(gelu_tanh, pre_f)
    grad_pre = pullback(by_token(gact_g).astype(F32))[0].astype(BF)
    return by_token(out_g), grad_pre, wg[None, 0:5], wg[5].T, wg[6]


def solution(mesh):
    whole = Mesh(mesh.devices.reshape(4, 8, 4, 2), ("x", "z", "y", "seq"))
    hid = ("x", "z", "y")
    tokens = P(hid + ("seq",), None)
    return jax.shard_map(
        on_device,
        mesh=whole,
        in_specs=(tokens, P(hid, None, None, None), P(hid, None), P(None, hid), tokens),
        out_specs=(tokens, tokens, P(hid, None, "seq", None), P(hid, "seq"), P("seq", hid)),
        check_vma=False,
    )
```

```python
import functools
import math

import jax
import jax.numpy as jnp
from jax import lax
from jax.experimental import pallas as pl
from jax.experimental.pallas import tpu as pltpu
from jax.sharding import Mesh
from jax.sharding import PartitionSpec as P

MESH = pl.DeviceIdType.MESH
BF, F32 = jnp.bfloat16, jnp.float32
GROUPS = 32
FACTOR = 1.0 / math.sqrt(1536)


def flip(value, bit):
    step = 1 << bit
    return value + step - 2 * step * lax.rem(lax.div(value, step), 2)


def dot(a, b):
    return jnp.dot(a, b, preferred_element_type=F32)


def dot_t(a, b):
    return lax.dot_general(a, b, (((1,), (1,)), ((), ())), preferred_element_type=F32)


def t_dot(a, b):
    return lax.dot_general(a, b, (((0,), (0,)), ((), ())), preferred_element_type=F32)


def cols(start, size, unit):
    return pl.ds(pl.multiple_of(start, unit), size)


CHANNELS = (
    "pre", "gin", "g", "a", "own", "zfar3", "zfar4", "g1", "g2", "gsib", "asib0", "asib1", "asib2", "farsib",
    "latz", "bcz", "latsib", "out", "gact", "a1h0", "a1h1", "a2h0", "a2h1",
) + tuple(
    name + str(d)
    for name in ("low", "lows", "fly", "flys", "far", "fars", "latx", "bcx", "wa", "wb", "wc")
    for d in (1, 2, 3)
)
CH = {name: i for i, name in enumerate(CHANNELS)}


def gelu_tanh(value):
    return jax.nn.gelu(value, approximate=True)


def kernel(
    pre_hbm, grad_hbm, bfly, low_u, low_v,
    out_ref, gp_ref, gb_ref, gu_ref, gv_ref,
    pre, grad_in, act, grad, out_tok, gact_tok, wg_own,
    A, G, DA, DG, DG1, DG2, W, acc_o, acc_g, stage, lat_send, latx_recv, latx, latz_recv,
    lat_own, lat_all, wg_send, wg_recv, send_sem, recv_sem,
):
    x, z, y, c = (lax.axis_index(n) for n in ("x", "z", "y", "seq"))
    me = x * 8 + z
    sib = 1 - c
    mine, other = cols(c * 128, 128, 128), cols(sib * 128, 128, 128)
    z1, z2 = flip(z, 0), flip(z, 1)

    def remote(src, dst, ch, **dev):
        pltpu.make_async_remote_copy(
            src_ref=src, dst_ref=dst, send_sem=send_sem.at[CH[ch]], recv_sem=recv_sem.at[CH[ch]],
            device_id=dev, device_id_type=MESH,
        ).start()

    def local(src, dst, ch):
        pltpu.make_async_copy(src, dst, recv_sem.at[CH[ch]]).start()

    def arrived(ref, ch):
        pltpu.make_async_copy(ref, ref, recv_sem.at[CH[ch]]).wait()

    def sent(ref, ch):
        pltpu.make_async_copy(ref, ref, send_sem.at[CH[ch]]).wait()

    def peer(d):
        q = lax.rem(me + d, GROUPS)
        return q, lax.div(q, 8), lax.rem(q, 8)

    def ypeer(d):
        return lax.rem(y + d, 4)

    def xpeer(d):
        return lax.rem(x + d, 4)

    def xrows(xv):
        return pl.ds(xv * 8, 8)

    local(pre_hbm, pre, "pre")
    local(grad_hbm, grad_in, "gin")

    barrier = pltpu.get_barrier_semaphore()

    @pl.loop(1, GROUPS)
    def _(d):
        q, qx, qz = peer(d)
        pl.semaphore_signal(barrier, 1, device_id={"x": qx, "z": qz}, device_id_type=MESH)

    for d in range(1, 4):
        pl.semaphore_signal(barrier, 1, device_id={"y": ypeer(d)}, device_id_type=MESH)
    pl.semaphore_signal(barrier, 1, device_id={"seq": sib}, device_id_type=MESH)

    arrived(grad_in, "gin")

    @pl.loop(0, GROUPS)
    def _(q):
        grad[q] = grad_in[:, cols(q * 1024, 1024, 1024)].reshape(3, 2, 1024)

    arrived(pre, "pre")
    pl.semaphore_wait(barrier, GROUPS + 3)

    def scatter(src, dst, ch):
        @pl.loop(1, GROUPS)
        def _(d):
            q, qx, qz = peer(d)
            remote(src.at[q], dst.at[me], ch, x=qx, z=qz)

        local(src.at[me], dst.at[me], ch)

    fly, low, far = pl.ds(0, 5), pl.ds(5, 2), pl.ds(7, 2)
    scatter(grad, G.at[0], "g")
    local(bfly, W.at[y, fly], "own")
    local(low_u, W.at[y, 5], "own")
    local(low_v, W.at[y, 6], "own")
    for d in range(1, 4):
        remote(low_u.at[mine], W.at[y, 5, mine], f"low{d}", y=ypeer(d))
        remote(low_v.at[mine], W.at[y, 6, mine], f"low{d}", y=ypeer(d))
    remote(bfly.at[3, mine], W.at[y, 7, mine], "zfar3", z=z1)
    remote(bfly.at[4, mine], W.at[y, 8, mine], "zfar4", z=z2)

    @pl.loop(0, GROUPS)
    def _(q):
        value = gelu_tanh(pre[:, cols(q * 1024, 1024, 1024)].astype(F32))
        act[q] = value.astype(BF).reshape(3, 2, 1024)

    scatter(act, A.at[0], "a")
    for d in range(1, 4):
        remote(bfly.at[:, mine], W.at[y, fly, mine], f"fly{d}", y=ypeer(d))

    for d in range(1, 4):
        ys = ypeer(4 - d)
        arrived(W.at[ys, low, mine], f"low{d}")
        remote(W.at[ys, low, mine], W.at[ys, low, mine], f"lows{d}", seq=sib)

    def dense(raw, out):
        @pl.loop(0, 4)
        def _(b):
            here = cols(b * 256, 256, 256)
            out[:, here] = raw[:, :, :, here].reshape(192, 256)

    arrived(G.at[0], "g")
    remote(G.at[0], G.at[2], "g2", z=z2)
    remote(G.at[0], G.at[1], "g1", z=z1)
    dense(G.at[0], DG.at[c])
    remote(DG.at[c], DG.at[c], "gsib", seq=sib)

    arrived(W.at[y, 7, mine], "zfar3")
    arrived(W.at[y, 8, mine], "zfar4")
    for d in range(1, 4):
        remote(W.at[y, far, mine], W.at[y, far, mine], f"far{d}", y=ypeer(d))
    remote(W.at[y, far, mine], W.at[y, far, mine], "farsib", seq=sib)

    arrived(A.at[0], "a")
    dense(A.at[0], DA.at[0, c])
    remote(DA.at[0, c], DA.at[0, c], "asib0", seq=sib)
    A0, G0 = DA.at[0, c], DG.at[c]

    arrived(W.at[y, pl.ds(0, 7)], "own")
    for d in range(1, 4):
        arrived(W.at[ypeer(4 - d), low, other], f"lows{d}")
    lat = dlat = None
    for b in range(4):
        u = dot(A0[:, b * 256 : b * 256 + 256], W[b, 5])
        v = dot_t(G0[:, b * 256 : b * 256 + 256], W[b, 6])
        lat, dlat = (u, v) if b == 0 else (lat + u, dlat + v)
    lat_send[:, :, :, 0:256] = lat.astype(BF).reshape(GROUPS, 3, 2, 256)
    lat_send[:, :, :, 256:512] = dlat.astype(BF).reshape(GROUPS, 3, 2, 256)
    for d in range(1, 4):
        remote(lat_send.at[xrows(xpeer(d))], latx_recv.at[d - 1], f"latx{d}", x=xpeer(d))

    for d in range(1, 4):
        ys = ypeer(4 - d)
        arrived(W.at[ys, fly, mine], f"fly{d}")
        remote(W.at[ys, fly, mine], W.at[ys, fly, mine], f"flys{d}", seq=sib)

    total = lat_send[xrows(x)].astype(F32)
    for d in range(1, 4):
        arrived(latx_recv.at[d - 1], f"latx{d}")
        total = total + latx_recv[d - 1].astype(F32)
    latx[...] = total.astype(BF)
    for d in range(1, 8):
        zp = lax.rem(z + d, 8)
        remote(latx.at[zp], latz_recv.at[z], "latz", z=zp)
    local(latx.at[z], latz_recv.at[z], "latz")

    first, second = pl.ds(0, 16), pl.ds(16, 16)
    remote(A.at[0, first], A.at[2, first], "a2h0", z=z2)
    remote(A.at[0, first], A.at[1, first], "a1h0", z=z1)

    for d in range(1, 4):
        arrived(W.at[ypeer(4 - d), fly, other], f"flys{d}")

    @pl.loop(0, 4)
    def _(b):
        b1, b2 = flip(b, 0), flip(b, 1)
        h0, h1, h2 = (cols(v * 256, 256, 256) for v in (b, b1, b2))
        acc_o[:, h0] = dot(A0[:, h0], W[b, 0]) + dot(A0[:, h1], W[b, 1]) + dot(A0[:, h2], W[b, 2])
        acc_g[:, h0] = (
            dot_t(G0[:, h0], W[b, 0]) + dot_t(G0[:, h1], W[b1, 1]) + dot_t(G0[:, h2], W[b2, 2])
        )

    arrived(latz_recv, "latz")
    total = latz_recv[0].astype(F32)
    for q in range(1, 8):
        total = total + latz_recv[q].astype(F32)
    lat_own[...] = total.astype(BF)
    for d in range(1, 8):
        remote(lat_own, lat_all.at[c, me], "bcz", z=lax.rem(z + d, 8))
    local(lat_own, lat_all.at[c, me], "bcz")
    remote(A.at[0, second], A.at[2, second], "a2h1", z=z2)
    remote(A.at[0, second], A.at[1, second], "a1h1", z=z1)

    def half(level, b):
        return DA[level, :, :, cols(b * 256 + c * 128, 128, 128)].reshape(384, 128)

    def gblock(b):
        return DG[:, :, cols(b * 256, 256, 256)].reshape(384, 256)

    def keep(d, k, value):
        if d == 0:
            wg_own[k] = value * FACTOR
        else:
            wg_send[d - 1, k] = (value * FACTOR).astype(BF)

    def ship(d, name, rows):
        if d:
            remote(wg_send.at[d - 1, rows], wg_recv.at[d - 1, rows], f"{name}{d}", y=ypeer(d))

    part_a, part_b, part_c = pl.ds(0, 3), pl.ds(5, 2), pl.ds(3, 2)
    arrived(DG.at[sib], "gsib")
    arrived(DA.at[0, sib], "asib0")
    for d in (2, 1, 3, 0):
        b = ypeer(d)
        g = gblock(b)
        keep(d, 0, t_dot(half(0, b), g))
        keep(d, 1, t_dot(half(0, flip(b, 0)), g))
        keep(d, 2, t_dot(half(0, flip(b, 1)), g))
        ship(d, "wa", part_a)

    for d in range(1, 4):
        ys = ypeer(4 - d)
        arrived(W.at[ys, far, mine], f"far{d}")
        remote(W.at[ys, far, mine], W.at[ys, far, mine], f"fars{d}", seq=sib)

    arrived(lat_all.at[c, xrows(x)], "bcz")
    for d in range(1, 4):
        rows = xrows(x)
        remote(lat_all.at[c, rows], lat_all.at[c, rows], f"bcx{d}", x=xpeer(d))

    arrived(G.at[1], "g1")
    dense(G.at[1], DG1)
    arrived(G.at[2], "g2")
    dense(G.at[2], DG2)
    arrived(W.at[y, far, other], "farsib")
    for d in range(1, 4):
        arrived(W.at[ypeer(4 - d), far, other], f"fars{d}")
    for d in range(1, 4):
        arrived(lat_all.at[c, xrows(xpeer(4 - d))], f"bcx{d}")
    remote(lat_all.at[c], lat_all.at[c], "latsib", seq=sib)
    pair = lat_all[c].reshape(192, 512)

    @pl.loop(0, 4)
    def _(b):
        here = cols(b * 256, 256, 256)
        g = (
            acc_g[:, here] + dot_t(DG1[:, here], W[b, 7]) + dot_t(DG2[:, here], W[b, 8])
            + dot_t(pair[:, 256:512], W[b, 5])
        )
        stage[1, :, :, :, here] = g.astype(BF).reshape(GROUPS, 3, 2, 256)

    def gather(which, ref, ch):
        @pl.loop(1, GROUPS)
        def _(d):
            q, qx, qz = peer(d)
            remote(stage.at[which, q], ref.at[me], ch, x=qx, z=qz)

        local(stage.at[which, me], ref.at[me], ch)

    gather(1, gact_tok, "gact")

    arrived(lat_all.at[sib], "latsib")
    lat_half = lat_all[:, :, :, :, cols(c * 128, 128, 128)].reshape(384, 128)
    dlat_half = lat_all[:, :, :, :, cols(256 + c * 128, 128, 128)].reshape(384, 128)
    for d in (2, 1, 3, 0):
        b = ypeer(d)
        keep(d, 5, t_dot(dlat_half, DA[0, :, :, cols(b * 256, 256, 256)].reshape(384, 256)))
        keep(d, 6, t_dot(lat_half, gblock(b)))
        ship(d, "wb", part_b)

    for half_rows, n in ((first, 0), (second, 1)):
        arrived(A.at[2, half_rows], f"a2h{n}")
        arrived(A.at[1, half_rows], f"a1h{n}")
    dense(A.at[1], DA.at[1, c])
    dense(A.at[2], DA.at[2, c])
    remote(DA.at[1, c], DA.at[1, c], "asib1", seq=sib)
    remote(DA.at[2, c], DA.at[2, c], "asib2", seq=sib)
    A1, A2 = DA.at[1, c], DA.at[2, c]

    @pl.loop(0, 4)
    def _(b):
        here = cols(b * 256, 256, 256)
        o = (
            acc_o[:, here] + dot(A1[:, here], W[b, 3]) + dot(A2[:, here], W[b, 4])
            + dot(pair[:, 0:256], W[b, 6])
        )
        stage[0, :, :, :, here] = o.astype(BF).reshape(GROUPS, 3, 2, 256)

    gather(0, out_tok, "out")

    arrived(DA.at[1, sib], "asib1")
    arrived(DA.at[2, sib], "asib2")
    for d in (2, 1, 3, 0):
        b = ypeer(d)
        g = gblock(b)
        keep(d, 3, t_dot(half(1, b), g))
        keep(d, 4, t_dot(half(2, b), g))
        ship(d, "wc", part_c)

    arrived(stage.at[1], "gact")

    @pl.loop(0, GROUPS)
    def _(q):
        here = cols(q * 1024, 1024, 1024)
        slope = jax.vjp(gelu_tanh, pre[:, here].astype(F32))[1]
        gp_ref[:, here] = slope(gact_tok[q].reshape(6, 1024).astype(F32))[0].astype(BF)

    def total_of(k):
        far_sum = wg_recv[0, k].astype(F32) + wg_recv[1, k].astype(F32)
        return wg_own[k] + far_sum + wg_recv[2, k].astype(F32)

    for name, rows in (("wa", part_a), ("wb", part_b), ("wc", part_c)):
        for d in range(1, 4):
            arrived(wg_recv.at[d - 1, rows], f"{name}{d}")
    for k in range(5):
        gb_ref[k] = total_of(k)
    gu_ref[...] = total_of(5).T
    gv_ref[...] = total_of(6)
    arrived(stage.at[0], "out")

    @pl.loop(0, GROUPS)
    def _(q):
        out_ref[:, cols(q * 1024, 1024, 1024)] = out_tok[q].reshape(6, 1024)

    most = pl.ds(0, GROUPS - 1)
    top = pl.ds(0, 128)
    sent(G.at[0, most], "g")
    sent(A.at[0, most], "a")
    sent(W.at[0, 7, top], "zfar3")
    sent(W.at[0, 8, top], "zfar4")
    sent(W.at[0, far, top], "farsib")
    for d in range(1, 4):
        sent(W.at[0, low, top], f"low{d}")
        sent(W.at[0, low, top], f"lows{d}")
        sent(W.at[0, fly, top], f"fly{d}")
        sent(W.at[0, fly, top], f"flys{d}")
        sent(W.at[0, far, top], f"far{d}")
        sent(W.at[0, far, top], f"fars{d}")
        sent(latx, f"latx{d}")
        sent(latx, f"bcx{d}")
        sent(wg_send.at[d - 1, part_a], f"wa{d}")
        sent(wg_send.at[d - 1, part_b], f"wb{d}")
        sent(wg_send.at[d - 1, part_c], f"wc{d}")
    sent(G.at[0], "g1")
    sent(G.at[0], "g2")
    for ch in ("gsib", "asib0", "asib1", "asib2"):
        sent(DG.at[0], ch)
    for ch in ("a1h0", "a1h1", "a2h0", "a2h1"):
        sent(A.at[0, first], ch)
    sent(latx.at[pl.ds(0, 7)], "latz")
    sent(latx.at[pl.ds(0, 7)], "bcz")
    sent(lat_all.at[0], "latsib")
    sent(stage.at[0, most], "out")
    sent(stage.at[1, most], "gact")


def exchange(pre_act, grad_out, bfly, low_u, low_v):
    tok = (GROUPS, 3, 2, 1024)
    any_space = pl.BlockSpec(memory_space=pl.ANY)
    vmem = pl.BlockSpec(memory_space=pltpu.VMEM)
    return pl.pallas_call(
        kernel,
        out_shape=(
            jax.ShapeDtypeStruct((6, 32768), BF),
            jax.ShapeDtypeStruct((6, 32768), BF),
            jax.ShapeDtypeStruct((5, 128, 256), F32),
            jax.ShapeDtypeStruct((256, 128), F32),
            jax.ShapeDtypeStruct((128, 256), F32),
        ),
        in_specs=[any_space] * 5,
        out_specs=(vmem,) * 5,
        scratch_shapes=[
            pltpu.VMEM((6, 32768), BF),
            pltpu.VMEM((6, 32768), BF),
            pltpu.VMEM(tok, BF),
            pltpu.VMEM(tok, BF),
            pltpu.VMEM(tok, BF),
            pltpu.VMEM(tok, BF),
            pltpu.VMEM((7, 128, 256), F32),
            pltpu.VMEM((3,) + tok, BF),
            pltpu.VMEM((3,) + tok, BF),
            pltpu.VMEM((3, 2, 192, 1024), BF),
            pltpu.VMEM((2, 192, 1024), BF),
            pltpu.VMEM((192, 1024), BF),
            pltpu.VMEM((192, 1024), BF),
            pltpu.VMEM((4, 9, 256, 256), BF),
            pltpu.VMEM((192, 1024), F32),
            pltpu.VMEM((192, 1024), F32),
            pltpu.VMEM((2,) + tok, BF),
            pltpu.VMEM((GROUPS, 3, 2, 512), BF),
            pltpu.VMEM((3, 8, 3, 2, 512), BF),
            pltpu.VMEM((8, 3, 2, 512), BF),
            pltpu.VMEM((8, 3, 2, 512), BF),
            pltpu.VMEM((3, 2, 512), BF),
            pltpu.VMEM((2, GROUPS, 3, 2, 512), BF),
            pltpu.VMEM((3, 7, 128, 256), BF),
            pltpu.VMEM((3, 7, 128, 256), BF),
            pltpu.SemaphoreType.DMA((len(CHANNELS),)),
            pltpu.SemaphoreType.DMA((len(CHANNELS),)),
        ],
        compiler_params=pltpu.CompilerParams(
            collective_id=0, has_side_effects=True, vmem_limit_bytes=67043328
        ),
    )(pre_act, grad_out, bfly, low_u, low_v)


def store_kernel(*refs):
    sources, targets, sem = refs[0:5], refs[5:10], refs[10]
    copies = [
        pltpu.make_async_copy(source, target, sem.at[i])
        for i, (source, target) in enumerate(zip(sources, targets))
    ]
    for copy in copies:
        copy.start()
    for copy in copies:
        copy.wait()


def store(*values):
    any_space = pl.BlockSpec(memory_space=pl.ANY)
    return pl.pallas_call(
        store_kernel,
        out_shape=tuple(jax.ShapeDtypeStruct(v.shape, v.dtype) for v in values),
        in_specs=[pl.BlockSpec(memory_space=pltpu.VMEM)] * 5,
        out_specs=(any_space,) * 5,
        scratch_shapes=[pltpu.SemaphoreType.DMA((5,))],
    )(*values)


def on_device(pre_act, butterfly, low_u, low_v, grad_out):
    parts = exchange(pre_act, grad_out, butterfly[0], low_u, low_v)
    out, grad_pre, gb, gu, gv = parts
    return out, grad_pre, gb[None], gu, gv


def solution(mesh):
    whole = Mesh(mesh.devices.reshape(4, 8, 4, 2), ("x", "z", "y", "seq"))
    hid = ("x", "z", "y")
    tokens = P(hid + ("seq",), None)
    return jax.shard_map(
        on_device,
        mesh=whole,
        in_specs=(tokens, P(hid, None, None, None), P(hid, None), P(None, hid), tokens),
        out_specs=(tokens, tokens, P(hid, None, "seq", None), P(hid, "seq"), P("seq", hid)),
        check_vma=False,
    )
```

```python
import functools
import math

import jax
import jax.numpy as jnp
from jax import lax
from jax.experimental import pallas as pl
from jax.experimental.pallas import tpu as pltpu
from jax.sharding import Mesh
from jax.sharding import PartitionSpec as P

MESH = pl.DeviceIdType.MESH
BF, F32 = jnp.bfloat16, jnp.float32
GROUPS = 32
FACTOR = 1.0 / math.sqrt(1536)


def flip(value, bit):
    step = 1 << bit
    return value + step - 2 * step * lax.rem(lax.div(value, step), 2)


def dot(a, b):
    return jnp.dot(a, b, preferred_element_type=F32)


def dot_t(a, b):
    return lax.dot_general(a, b, (((1,), (1,)), ((), ())), preferred_element_type=F32)


def t_dot(a, b):
    return lax.dot_general(a, b, (((0,), (0,)), ((), ())), preferred_element_type=F32)


def cols(start, size, unit):
    return pl.ds(pl.multiple_of(start, unit), size)


CHANNELS = (
    "pre", "gin", "g", "a", "own", "zfar3", "zfar4", "g1", "g2", "gsib", "asib0", "asib1", "asib2", "farsib",
    "latz", "bcz", "latsib", "out", "gact", "a1h0", "a1h1", "a2h0", "a2h1",
) + tuple(
    name + str(d)
    for name in ("low", "lows", "fly", "flys", "far", "fars", "latx", "bcx", "wa", "wb", "wc")
    for d in (1, 2, 3)
)
CH = {name: i for i, name in enumerate(CHANNELS)}


def gelu_tanh(value):
    return jax.nn.gelu(value, approximate=True)


def kernel(
    pre_hbm, grad_hbm, bfly, low_u, low_v,
    out_ref, gp_ref, gb_ref, gu_ref, gv_ref,
    pre, grad_in, act, grad, out_tok, gact_tok, wg_own,
    A, G, DA, DG, DG1, DG2, W, acc_o, acc_g, stage, lat_send, latx_recv, latx, latz_recv,
    lat_own, lat_all, wg_send, wg_recv, send_sem, recv_sem,
):
    x, z, y, c = (lax.axis_index(n) for n in ("x", "z", "y", "seq"))
    me = x * 8 + z
    sib = 1 - c
    mine, other = cols(c * 128, 128, 128), cols(sib * 128, 128, 128)
    z1, z2 = flip(z, 0), flip(z, 1)

    def remote(src, dst, ch, **dev):
        pltpu.make_async_remote_copy(
            src_ref=src, dst_ref=dst, send_sem=send_sem.at[CH[ch]], recv_sem=recv_sem.at[CH[ch]],
            device_id=dev, device_id_type=MESH,
        ).start()

    def local(src, dst, ch):
        pltpu.make_async_copy(src, dst, recv_sem.at[CH[ch]]).start()

    def arrived(ref, ch):
        pltpu.make_async_copy(ref, ref, recv_sem.at[CH[ch]]).wait()

    def sent(ref, ch):
        pltpu.make_async_copy(ref, ref, send_sem.at[CH[ch]]).wait()

    def peer(d):
        q = lax.rem(me + d, GROUPS)
        return q, lax.div(q, 8), lax.rem(q, 8)

    def ypeer(d):
        return lax.rem(y + d, 4)

    def xpeer(d):
        return lax.rem(x + d, 4)

    def xrows(xv):
        return pl.ds(xv * 8, 8)

    local(pre_hbm, pre, "pre")
    local(grad_hbm, grad_in, "gin")

    barrier = pltpu.get_barrier_semaphore()

    @pl.loop(1, GROUPS)
    def _(d):
        q, qx, qz = peer(d)
        pl.semaphore_signal(barrier, 1, device_id={"x": qx, "z": qz}, device_id_type=MESH)

    for d in range(1, 4):
        pl.semaphore_signal(barrier, 1, device_id={"y": ypeer(d)}, device_id_type=MESH)
    pl.semaphore_signal(barrier, 1, device_id={"seq": sib}, device_id_type=MESH)

    arrived(grad_in, "gin")

    @pl.loop(0, GROUPS)
    def _(q):
        grad[q] = grad_in[:, cols(q * 1024, 1024, 1024)].reshape(3, 2, 1024)

    arrived(pre, "pre")
    pl.semaphore_wait(barrier, GROUPS + 3)

    def scatter(src, dst, ch):
        @pl.loop(1, GROUPS)
        def _(d):
            q, qx, qz = peer(d)
            remote(src.at[q], dst.at[me], ch, x=qx, z=qz)

        local(src.at[me], dst.at[me], ch)

    fly, low, far = pl.ds(0, 5), pl.ds(5, 2), pl.ds(7, 2)
    scatter(grad, G.at[0], "g")
    local(bfly, W.at[y, fly], "own")
    local(low_u, W.at[y, 5], "own")
    local(low_v, W.at[y, 6], "own")
    for d in range(1, 4):
        remote(low_u.at[mine], W.at[y, 5, mine], f"low{d}", y=ypeer(d))
        remote(low_v.at[mine], W.at[y, 6, mine], f"low{d}", y=ypeer(d))
    remote(bfly.at[3, mine], W.at[y, 7, mine], "zfar3", z=z1)
    remote(bfly.at[4, mine], W.at[y, 8, mine], "zfar4", z=z2)

    @pl.loop(0, GROUPS)
    def _(q):
        value = gelu_tanh(pre[:, cols(q * 1024, 1024, 1024)].astype(F32))
        act[q] = value.astype(BF).reshape(3, 2, 1024)

    scatter(act, A.at[0], "a")
    for d in range(1, 4):
        remote(bfly.at[:, mine], W.at[y, fly, mine], f"fly{d}", y=ypeer(d))

    for d in range(1, 4):
        ys = ypeer(4 - d)
        arrived(W.at[ys, low, mine], f"low{d}")
        remote(W.at[ys, low, mine], W.at[ys, low, mine], f"lows{d}", seq=sib)

    def dense(raw, out):
        @pl.loop(0, 4)
        def _(b):
            here = cols(b * 256, 256, 256)
            out[:, here] = raw[:, :, :, here].reshape(192, 256)

    arrived(G.at[0], "g")
    remote(G.at[0], G.at[2], "g2", z=z2)
    remote(G.at[0], G.at[1], "g1", z=z1)
    dense(G.at[0], DG.at[c])
    remote(DG.at[c], DG.at[c], "gsib", seq=sib)

    arrived(W.at[y, 7, mine], "zfar3")
    arrived(W.at[y, 8, mine], "zfar4")
    for d in range(1, 4):
        remote(W.at[y, far, mine], W.at[y, far, mine], f"far{d}", y=ypeer(d))
    remote(W.at[y, far, mine], W.at[y, far, mine], "farsib", seq=sib)

    arrived(A.at[0], "a")
    dense(A.at[0], DA.at[0, c])
    remote(DA.at[0, c], DA.at[0, c], "asib0", seq=sib)
    A0, G0 = DA.at[0, c], DG.at[c]

    arrived(W.at[y, pl.ds(0, 7)], "own")
    for d in range(1, 4):
        arrived(W.at[ypeer(4 - d), low, other], f"lows{d}")
    lat = dlat = None
    for b in range(4):
        u = dot(A0[:, b * 256 : b * 256 + 256], W[b, 5])
        v = dot_t(G0[:, b * 256 : b * 256 + 256], W[b, 6])
        lat, dlat = (u, v) if b == 0 else (lat + u, dlat + v)
    lat_send[:, :, :, 0:256] = lat.astype(BF).reshape(GROUPS, 3, 2, 256)
    lat_send[:, :, :, 256:512] = dlat.astype(BF).reshape(GROUPS, 3, 2, 256)
    for d in range(1, 4):
        remote(lat_send.at[xrows(xpeer(d))], latx_recv.at[d - 1], f"latx{d}", x=xpeer(d))

    for d in range(1, 4):
        ys = ypeer(4 - d)
        arrived(W.at[ys, fly, mine], f"fly{d}")
        remote(W.at[ys, fly, mine], W.at[ys, fly, mine], f"flys{d}", seq=sib)

    total = lat_send[xrows(x)].astype(F32)
    for d in range(1, 4):
        arrived(latx_recv.at[d - 1], f"latx{d}")
        total = total + latx_recv[d - 1].astype(F32)
    latx[...] = total.astype(BF)
    for d in range(1, 8):
        zp = lax.rem(z + d, 8)
        remote(latx.at[zp], latz_recv.at[z], "latz", z=zp)
    local(latx.at[z], latz_recv.at[z], "latz")

    first, second = pl.ds(0, 16), pl.ds(16, 16)
    remote(A.at[0, first], A.at[2, first], "a2h0", z=z2)
    remote(A.at[0, first], A.at[1, first], "a1h0", z=z1)

    for d in range(1, 4):
        arrived(W.at[ypeer(4 - d), fly, other], f"flys{d}")

    @pl.loop(0, 4)
    def _(b):
        b1, b2 = flip(b, 0), flip(b, 1)
        h0, h1, h2 = (cols(v * 256, 256, 256) for v in (b, b1, b2))
        acc_o[:, h0] = dot(A0[:, h0], W[b, 0]) + dot(A0[:, h1], W[b, 1]) + dot(A0[:, h2], W[b, 2])
        acc_g[:, h0] = (
            dot_t(G0[:, h0], W[b, 0]) + dot_t(G0[:, h1], W[b1, 1]) + dot_t(G0[:, h2], W[b2, 2])
        )

    arrived(latz_recv, "latz")
    total = latz_recv[0].astype(F32)
    for q in range(1, 8):
        total = total + latz_recv[q].astype(F32)
    lat_own[...] = total.astype(BF)
    for d in range(1, 8):
        remote(lat_own, lat_all.at[c, me], "bcz", z=lax.rem(z + d, 8))
    local(lat_own, lat_all.at[c, me], "bcz")
    remote(A.at[0, second], A.at[2, second], "a2h1", z=z2)
    remote(A.at[0, second], A.at[1, second], "a1h1", z=z1)

    def half(level, b):
        return DA[level, :, :, cols(b * 256 + c * 128, 128, 128)].reshape(384, 128)

    def gblock(b):
        return DG[:, :, cols(b * 256, 256, 256)].reshape(384, 256)

    def keep(d, k, value):
        if d == 0:
            wg_own[k] = value * FACTOR
        else:
            wg_send[d - 1, k] = (value * FACTOR).astype(BF)

    def ship(d, name, rows):
        if d:
            remote(wg_send.at[d - 1, rows], wg_recv.at[d - 1, rows], f"{name}{d}", y=ypeer(d))

    part_a, part_b, part_c = pl.ds(0, 3), pl.ds(5, 2), pl.ds(3, 2)
    arrived(DG.at[sib], "gsib")
    arrived(DA.at[0, sib], "asib0")
    for d in (2, 1, 3, 0):
        b = ypeer(d)
        g = gblock(b)
        keep(d, 0, t_dot(half(0, b), g))
        keep(d, 1, t_dot(half(0, flip(b, 0)), g))
        keep(d, 2, t_dot(half(0, flip(b, 1)), g))
        ship(d, "wa", part_a)

    for d in range(1, 4):
        ys = ypeer(4 - d)
        arrived(W.at[ys, far, mine], f"far{d}")
        remote(W.at[ys, far, mine], W.at[ys, far, mine], f"fars{d}", seq=sib)

    arrived(lat_all.at[c, xrows(x)], "bcz")
    for d in range(1, 4):
        rows = xrows(x)
        remote(lat_all.at[c, rows], lat_all.at[c, rows], f"bcx{d}", x=xpeer(d))

    arrived(G.at[1], "g1")
    dense(G.at[1], DG1)
    arrived(G.at[2], "g2")
    dense(G.at[2], DG2)
    arrived(W.at[y, far, other], "farsib")
    for d in range(1, 4):
        arrived(W.at[ypeer(4 - d), far, other], f"fars{d}")
    for d in range(1, 4):
        arrived(lat_all.at[c, xrows(xpeer(4 - d))], f"bcx{d}")
    remote(lat_all.at[c], lat_all.at[c], "latsib", seq=sib)
    pair = lat_all[c].reshape(192, 512)

    @pl.loop(0, 4)
    def _(b):
        here = cols(b * 256, 256, 256)
        g = (
            acc_g[:, here] + dot_t(DG1[:, here], W[b, 7]) + dot_t(DG2[:, here], W[b, 8])
            + dot_t(pair[:, 256:512], W[b, 5])
        )
        stage[1, :, :, :, here] = g.astype(BF).reshape(GROUPS, 3, 2, 256)

    def gather(which, ref, ch):
        @pl.loop(1, GROUPS)
        def _(d):
            q, qx, qz = peer(d)
            remote(stage.at[which, q], ref.at[me], ch, x=qx, z=qz)

        local(stage.at[which, me], ref.at[me], ch)

    gather(1, gact_tok, "gact")

    arrived(lat_all.at[sib], "latsib")
    lat_half = lat_all[:, :, :, :, cols(c * 128, 128, 128)].reshape(384, 128)
    dlat_half = lat_all[:, :, :, :, cols(256 + c * 128, 128, 128)].reshape(384, 128)
    for d in (2, 1, 3, 0):
        b = ypeer(d)
        keep(d, 5, t_dot(dlat_half, DA[0, :, :, cols(b * 256, 256, 256)].reshape(384, 256)))
        keep(d, 6, t_dot(lat_half, gblock(b)))
        ship(d, "wb", part_b)

    for half_rows, n in ((first, 0), (second, 1)):
        arrived(A.at[2, half_rows], f"a2h{n}")
        arrived(A.at[1, half_rows], f"a1h{n}")
    dense(A.at[1], DA.at[1, c])
    dense(A.at[2], DA.at[2, c])
    remote(DA.at[1, c], DA.at[1, c], "asib1", seq=sib)
    remote(DA.at[2, c], DA.at[2, c], "asib2", seq=sib)
    A1, A2 = DA.at[1, c], DA.at[2, c]

    @pl.loop(0, 4)
    def _(b):
        here = cols(b * 256, 256, 256)
        o = (
            acc_o[:, here] + dot(A1[:, here], W[b, 3]) + dot(A2[:, here], W[b, 4])
            + dot(pair[:, 0:256], W[b, 6])
        )
        stage[0, :, :, :, here] = o.astype(BF).reshape(GROUPS, 3, 2, 256)

    gather(0, out_tok, "out")

    arrived(DA.at[1, sib], "asib1")
    arrived(DA.at[2, sib], "asib2")
    for d in (2, 1, 3, 0):
        b = ypeer(d)
        g = gblock(b)
        keep(d, 3, t_dot(half(1, b), g))
        keep(d, 4, t_dot(half(2, b), g))
        ship(d, "wc", part_c)

    arrived(stage.at[1], "gact")

    @pl.loop(0, GROUPS)
    def _(q):
        here = cols(q * 1024, 1024, 1024)
        slope = jax.vjp(gelu_tanh, pre[:, here].astype(F32))[1]
        gp_ref[:, here] = slope(gact_tok[q].reshape(6, 1024).astype(F32))[0].astype(BF)

    def total_of(k):
        far_sum = wg_recv[0, k].astype(F32) + wg_recv[1, k].astype(F32)
        return wg_own[k] + far_sum + wg_recv[2, k].astype(F32)

    for name, rows in (("wa", part_a), ("wb", part_b), ("wc", part_c)):
        for d in range(1, 4):
            arrived(wg_recv.at[d - 1, rows], f"{name}{d}")
    for k in range(5):
        gb_ref[k] = total_of(k)
    gu_ref[...] = total_of(5).T
    gv_ref[...] = total_of(6)
    arrived(stage.at[0], "out")

    @pl.loop(0, GROUPS)
    def _(q):
        out_ref[:, cols(q * 1024, 1024, 1024)] = out_tok[q].reshape(6, 1024)

    most = pl.ds(0, GROUPS - 1)
    top = pl.ds(0, 128)
    sent(G.at[0, most], "g")
    sent(A.at[0, most], "a")
    sent(W.at[0, 7, top], "zfar3")
    sent(W.at[0, 8, top], "zfar4")
    sent(W.at[0, far, top], "farsib")
    for d in range(1, 4):
        sent(W.at[0, low, top], f"low{d}")
        sent(W.at[0, low, top], f"lows{d}")
        sent(W.at[0, fly, top], f"fly{d}")
        sent(W.at[0, fly, top], f"flys{d}")
        sent(W.at[0, far, top], f"far{d}")
        sent(W.at[0, far, top], f"fars{d}")
        sent(latx, f"latx{d}")
        sent(latx, f"bcx{d}")
        sent(wg_send.at[d - 1, part_a], f"wa{d}")
        sent(wg_send.at[d - 1, part_b], f"wb{d}")
        sent(wg_send.at[d - 1, part_c], f"wc{d}")
    sent(G.at[0], "g1")
    sent(G.at[0], "g2")
    for ch in ("gsib", "asib0", "asib1", "asib2"):
        sent(DG.at[0], ch)
    for ch in ("a1h0", "a1h1", "a2h0", "a2h1"):
        sent(A.at[0, first], ch)
    sent(latx.at[pl.ds(0, 7)], "latz")
    sent(latx.at[pl.ds(0, 7)], "bcz")
    sent(lat_all.at[0], "latsib")
    sent(stage.at[0, most], "out")
    sent(stage.at[1, most], "gact")


def exchange(pre_act, grad_out, bfly, low_u, low_v):
    tok = (GROUPS, 3, 2, 1024)
    any_space = pl.BlockSpec(memory_space=pl.ANY)
    vmem = pl.BlockSpec(memory_space=pltpu.VMEM)
    return pl.pallas_call(
        kernel,
        out_shape=(
            jax.ShapeDtypeStruct((6, 32768), BF),
            jax.ShapeDtypeStruct((6, 32768), BF),
            jax.ShapeDtypeStruct((5, 128, 256), F32),
            jax.ShapeDtypeStruct((256, 128), F32),
            jax.ShapeDtypeStruct((128, 256), F32),
        ),
        in_specs=[any_space] * 5,
        out_specs=(vmem,) * 5,
        scratch_shapes=[
            pltpu.VMEM((6, 32768), BF),
            pltpu.VMEM((6, 32768), BF),
            pltpu.VMEM(tok, BF),
            pltpu.VMEM(tok, BF),
            pltpu.VMEM(tok, BF),
            pltpu.VMEM(tok, BF),
            pltpu.VMEM((7, 128, 256), F32),
            pltpu.VMEM((3,) + tok, BF),
            pltpu.VMEM((3,) + tok, BF),
            pltpu.VMEM((3, 2, 192, 1024), BF),
            pltpu.VMEM((2, 192, 1024), BF),
            pltpu.VMEM((192, 1024), BF),
            pltpu.VMEM((192, 1024), BF),
            pltpu.VMEM((4, 9, 256, 256), BF),
            pltpu.VMEM((192, 1024), F32),
            pltpu.VMEM((192, 1024), F32),
            pltpu.VMEM((2,) + tok, BF),
            pltpu.VMEM((GROUPS, 3, 2, 512), BF),
            pltpu.VMEM((3, 8, 3, 2, 512), BF),
            pltpu.VMEM((8, 3, 2, 512), BF),
            pltpu.VMEM((8, 3, 2, 512), BF),
            pltpu.VMEM((3, 2, 512), BF),
            pltpu.VMEM((2, GROUPS, 3, 2, 512), BF),
            pltpu.VMEM((3, 7, 128, 256), BF),
            pltpu.VMEM((3, 7, 128, 256), BF),
            pltpu.SemaphoreType.DMA((len(CHANNELS),)),
            pltpu.SemaphoreType.DMA((len(CHANNELS),)),
        ],
        compiler_params=pltpu.CompilerParams(
            collective_id=0, has_side_effects=True, vmem_limit_bytes=48 * 2**20
        ),
    )(*(pltpu.with_memory_space_constraint(v, pltpu.HBM) for v in (pre_act, grad_out, bfly, low_u, low_v)))


def store_kernel(*refs):
    sources, targets, sem = refs[0:5], refs[5:10], refs[10]
    copies = [
        pltpu.make_async_copy(source, target, sem.at[i])
        for i, (source, target) in enumerate(zip(sources, targets))
    ]
    for copy in copies:
        copy.start()
    for copy in copies:
        copy.wait()


def store(*values):
    any_space = pl.BlockSpec(memory_space=pl.ANY)
    return pl.pallas_call(
        store_kernel,
        out_shape=tuple(jax.ShapeDtypeStruct(v.shape, v.dtype) for v in values),
        in_specs=[pl.BlockSpec(memory_space=pltpu.VMEM)] * 5,
        out_specs=(any_space,) * 5,
        scratch_shapes=[pltpu.SemaphoreType.DMA((5,))],
    )(*values)


def on_device(pre_act, butterfly, low_u, low_v, grad_out):
    parts = exchange(pre_act, grad_out, butterfly[0], low_u, low_v)
    out, grad_pre, gb, gu, gv = parts
    return out, grad_pre, gb[None], gu, gv


def solution(mesh):
    whole = Mesh(mesh.devices.reshape(4, 8, 4, 2), ("x", "z", "y", "seq"))
    hid = ("x", "z", "y")
    tokens = P(hid + ("seq",), None)
    return jax.shard_map(
        on_device,
        mesh=whole,
        in_specs=(tokens, P(hid, None, None, None), P(hid, None), P(None, hid), tokens),
        out_specs=(tokens, tokens, P(hid, None, "seq", None), P(hid, "seq"), P("seq", hid)),
        check_vma=False,
    )
```

```python
import functools
import math

import jax
import jax.numpy as jnp
from jax import lax
from jax.experimental import pallas as pl
from jax.experimental.pallas import tpu as pltpu
from jax.sharding import Mesh
from jax.sharding import PartitionSpec as P

MESH = pl.DeviceIdType.MESH
BF, F32 = jnp.bfloat16, jnp.float32
GROUPS = 32
FACTOR = 1.0 / math.sqrt(1536)


def flip(value, bit):
    step = 1 << bit
    return value + step - 2 * step * lax.rem(lax.div(value, step), 2)


def dot(a, b):
    return jnp.dot(a, b, preferred_element_type=F32)


def dot_t(a, b):
    return lax.dot_general(a, b, (((1,), (1,)), ((), ())), preferred_element_type=F32)


def t_dot(a, b):
    return lax.dot_general(a, b, (((0,), (0,)), ((), ())), preferred_element_type=F32)


def cols(start, size, unit):
    return pl.ds(pl.multiple_of(start, unit), size)


CHANNELS = (
    "pre", "gin", "g", "a", "own", "zfar3", "zfar4", "g1", "g2", "gsib", "asib0", "asib1", "asib2", "farsib",
    "latz", "bcz", "latsib", "out", "gact", "a1h0", "a1h1", "a2h0", "a2h1",
) + tuple(
    name + str(d)
    for name in ("low", "lows", "fly", "flys", "far", "fars", "latx", "bcx", "wa", "wb", "wc")
    for d in (1, 2, 3)
)
CH = {name: i for i, name in enumerate(CHANNELS)}


def gelu_tanh(value):
    return jax.nn.gelu(value, approximate=True)


def kernel(
    pre_hbm, grad_hbm, bfly, low_u, low_v,
    out_ref, gp_ref, gb_ref, gu_ref, gv_ref,
    pre, grad_in, act, grad, out_tok, gact_tok, wg_own,
    A, G, DA, DG, DG1, DG2, W, acc_o, acc_g, stage, lat_send, latx_recv, latx, latz_recv,
    lat_own, lat_all, wg_send, wg_recv, send_sem, recv_sem,
):
    x, z, y, c = (lax.axis_index(n) for n in ("x", "z", "y", "seq"))
    me = x * 8 + z
    sib = 1 - c
    mine, other = cols(c * 128, 128, 128), cols(sib * 128, 128, 128)
    z1, z2 = flip(z, 0), flip(z, 1)

    def remote(src, dst, ch, **dev):
        pltpu.make_async_remote_copy(
            src_ref=src, dst_ref=dst, send_sem=send_sem.at[CH[ch]], recv_sem=recv_sem.at[CH[ch]],
            device_id=dev, device_id_type=MESH,
        ).start()

    def local(src, dst, ch):
        pltpu.make_async_copy(src, dst, recv_sem.at[CH[ch]]).start()

    def arrived(ref, ch):
        pltpu.make_async_copy(ref, ref, recv_sem.at[CH[ch]]).wait()

    def sent(ref, ch):
        pltpu.make_async_copy(ref, ref, send_sem.at[CH[ch]]).wait()

    def peer(d):
        q = lax.rem(me + d, GROUPS)
        return q, lax.div(q, 8), lax.rem(q, 8)

    def ypeer(d):
        return lax.rem(y + d, 4)

    def xpeer(d):
        return lax.rem(x + d, 4)

    def xrows(xv):
        return pl.ds(xv * 8, 8)

    local(pre_hbm, pre, "pre")
    local(grad_hbm, grad_in, "gin")

    barrier = pltpu.get_barrier_semaphore()

    @pl.loop(1, GROUPS)
    def _(d):
        q, qx, qz = peer(d)
        pl.semaphore_signal(barrier, 1, device_id={"x": qx, "z": qz}, device_id_type=MESH)

    for d in range(1, 4):
        pl.semaphore_signal(barrier, 1, device_id={"y": ypeer(d)}, device_id_type=MESH)
    pl.semaphore_signal(barrier, 1, device_id={"seq": sib}, device_id_type=MESH)

    arrived(grad_in, "gin")

    @pl.loop(0, GROUPS, unroll=4)
    def _(q):
        grad[q] = grad_in[:, cols(q * 1024, 1024, 1024)].reshape(3, 2, 1024)

    arrived(pre, "pre")
    pl.semaphore_wait(barrier, GROUPS + 3)

    def scatter(src, dst, ch):
        @pl.loop(1, GROUPS)
        def _(d):
            q, qx, qz = peer(d)
            remote(src.at[q], dst.at[me], ch, x=qx, z=qz)

        local(src.at[me], dst.at[me], ch)

    fly, low, far = pl.ds(0, 5), pl.ds(5, 2), pl.ds(7, 2)
    scatter(grad, G.at[0], "g")
    local(bfly, W.at[y, fly], "own")
    local(low_u, W.at[y, 5], "own")
    local(low_v, W.at[y, 6], "own")
    for d in range(1, 4):
        remote(low_u.at[mine], W.at[y, 5, mine], f"low{d}", y=ypeer(d))
        remote(low_v.at[mine], W.at[y, 6, mine], f"low{d}", y=ypeer(d))
    remote(bfly.at[3, mine], W.at[y, 7, mine], "zfar3", z=z1)
    remote(bfly.at[4, mine], W.at[y, 8, mine], "zfar4", z=z2)

    @pl.loop(0, GROUPS, unroll=4)
    def _(q):
        value = gelu_tanh(pre[:, cols(q * 1024, 1024, 1024)].astype(F32))
        act[q] = value.astype(BF).reshape(3, 2, 1024)

    scatter(act, A.at[0], "a")
    for d in range(1, 4):
        remote(bfly.at[:, mine], W.at[y, fly, mine], f"fly{d}", y=ypeer(d))

    for d in range(1, 4):
        ys = ypeer(4 - d)
        arrived(W.at[ys, low, mine], f"low{d}")
        remote(W.at[ys, low, mine], W.at[ys, low, mine], f"lows{d}", seq=sib)

    def dense(raw, out):
        @pl.loop(0, 4)
        def _(b):
            here = cols(b * 256, 256, 256)
            out[:, here] = raw[:, :, :, here].reshape(192, 256)

    arrived(G.at[0], "g")
    remote(G.at[0], G.at[2], "g2", z=z2)
    remote(G.at[0], G.at[1], "g1", z=z1)
    dense(G.at[0], DG.at[c])
    remote(DG.at[c], DG.at[c], "gsib", seq=sib)

    arrived(W.at[y, 7, mine], "zfar3")
    arrived(W.at[y, 8, mine], "zfar4")
    for d in range(1, 4):
        remote(W.at[y, far, mine], W.at[y, far, mine], f"far{d}", y=ypeer(d))
    remote(W.at[y, far, mine], W.at[y, far, mine], "farsib", seq=sib)

    arrived(A.at[0], "a")
    dense(A.at[0], DA.at[0, c])
    remote(DA.at[0, c], DA.at[0, c], "asib0", seq=sib)
    A0, G0 = DA.at[0, c], DG.at[c]

    arrived(W.at[y, pl.ds(0, 7)], "own")
    for d in range(1, 4):
        arrived(W.at[ypeer(4 - d), low, other], f"lows{d}")
    lat = dlat = None
    for b in range(4):
        u = dot(A0[:, b * 256 : b * 256 + 256], W[b, 5])
        v = dot_t(G0[:, b * 256 : b * 256 + 256], W[b, 6])
        lat, dlat = (u, v) if b == 0 else (lat + u, dlat + v)
    lat_send[:, :, :, 0:256] = lat.astype(BF).reshape(GROUPS, 3, 2, 256)
    lat_send[:, :, :, 256:512] = dlat.astype(BF).reshape(GROUPS, 3, 2, 256)
    for d in range(1, 4):
        remote(lat_send.at[xrows(xpeer(d))], latx_recv.at[d - 1], f"latx{d}", x=xpeer(d))

    for d in range(1, 4):
        ys = ypeer(4 - d)
        arrived(W.at[ys, fly, mine], f"fly{d}")
        remote(W.at[ys, fly, mine], W.at[ys, fly, mine], f"flys{d}", seq=sib)

    total = lat_send[xrows(x)].astype(F32)
    for d in range(1, 4):
        arrived(latx_recv.at[d - 1], f"latx{d}")
        total = total + latx_recv[d - 1].astype(F32)
    latx[...] = total.astype(BF)
    for d in range(1, 8):
        zp = lax.rem(z + d, 8)
        remote(latx.at[zp], latz_recv.at[z], "latz", z=zp)
    local(latx.at[z], latz_recv.at[z], "latz")

    first, second = pl.ds(0, 16), pl.ds(16, 16)
    remote(A.at[0, first], A.at[2, first], "a2h0", z=z2)
    remote(A.at[0, first], A.at[1, first], "a1h0", z=z1)

    for d in range(1, 4):
        arrived(W.at[ypeer(4 - d), fly, other], f"flys{d}")

    @pl.loop(0, 4)
    def _(b):
        b1, b2 = flip(b, 0), flip(b, 1)
        h0, h1, h2 = (cols(v * 256, 256, 256) for v in (b, b1, b2))
        acc_o[:, h0] = dot(A0[:, h0], W[b, 0]) + dot(A0[:, h1], W[b, 1]) + dot(A0[:, h2], W[b, 2])
        acc_g[:, h0] = (
            dot_t(G0[:, h0], W[b, 0]) + dot_t(G0[:, h1], W[b1, 1]) + dot_t(G0[:, h2], W[b2, 2])
        )

    arrived(latz_recv, "latz")
    total = latz_recv[0].astype(F32)
    for q in range(1, 8):
        total = total + latz_recv[q].astype(F32)
    lat_own[...] = total.astype(BF)
    for d in range(1, 8):
        remote(lat_own, lat_all.at[c, me], "bcz", z=lax.rem(z + d, 8))
    local(lat_own, lat_all.at[c, me], "bcz")
    remote(A.at[0, second], A.at[2, second], "a2h1", z=z2)
    remote(A.at[0, second], A.at[1, second], "a1h1", z=z1)

    def half(level, b):
        return DA[level, :, :, cols(b * 256 + c * 128, 128, 128)].reshape(384, 128)

    def gblock(b):
        return DG[:, :, cols(b * 256, 256, 256)].reshape(384, 256)

    def keep(d, k, value):
        if d == 0:
            wg_own[k] = value * FACTOR
        else:
            wg_send[d - 1, k] = (value * FACTOR).astype(BF)

    def ship(d, name, rows):
        if d:
            remote(wg_send.at[d - 1, rows], wg_recv.at[d - 1, rows], f"{name}{d}", y=ypeer(d))

    part_a, part_b, part_c = pl.ds(0, 3), pl.ds(5, 2), pl.ds(3, 2)
    arrived(DG.at[sib], "gsib")
    arrived(DA.at[0, sib], "asib0")
    for d in (2, 1, 3, 0):
        b = ypeer(d)
        g = gblock(b)
        keep(d, 0, t_dot(half(0, b), g))
        keep(d, 1, t_dot(half(0, flip(b, 0)), g))
        keep(d, 2, t_dot(half(0, flip(b, 1)), g))
        ship(d, "wa", part_a)

    for d in range(1, 4):
        ys = ypeer(4 - d)
        arrived(W.at[ys, far, mine], f"far{d}")
        remote(W.at[ys, far, mine], W.at[ys, far, mine], f"fars{d}", seq=sib)

    arrived(lat_all.at[c, xrows(x)], "bcz")
    for d in range(1, 4):
        rows = xrows(x)
        remote(lat_all.at[c, rows], lat_all.at[c, rows], f"bcx{d}", x=xpeer(d))

    arrived(G.at[1], "g1")
    dense(G.at[1], DG1)
    arrived(G.at[2], "g2")
    dense(G.at[2], DG2)
    arrived(W.at[y, far, other], "farsib")
    for d in range(1, 4):
        arrived(W.at[ypeer(4 - d), far, other], f"fars{d}")
    for d in range(1, 4):
        arrived(lat_all.at[c, xrows(xpeer(4 - d))], f"bcx{d}")
    remote(lat_all.at[c], lat_all.at[c], "latsib", seq=sib)
    pair = lat_all[c].reshape(192, 512)

    @pl.loop(0, 4)
    def _(b):
        here = cols(b * 256, 256, 256)
        g = (
            acc_g[:, here] + dot_t(DG1[:, here], W[b, 7]) + dot_t(DG2[:, here], W[b, 8])
            + dot_t(pair[:, 256:512], W[b, 5])
        )
        stage[1, :, :, :, here] = g.astype(BF).reshape(GROUPS, 3, 2, 256)

    def gather(which, ref, ch):
        @pl.loop(1, GROUPS)
        def _(d):
            q, qx, qz = peer(d)
            remote(stage.at[which, q], ref.at[me], ch, x=qx, z=qz)

        local(stage.at[which, me], ref.at[me], ch)

    gather(1, gact_tok, "gact")

    arrived(lat_all.at[sib], "latsib")
    lat_half = lat_all[:, :, :, :, cols(c * 128, 128, 128)].reshape(384, 128)
    dlat_half = lat_all[:, :, :, :, cols(256 + c * 128, 128, 128)].reshape(384, 128)
    for d in (2, 1, 3, 0):
        b = ypeer(d)
        keep(d, 5, t_dot(dlat_half, DA[0, :, :, cols(b * 256, 256, 256)].reshape(384, 256)))
        keep(d, 6, t_dot(lat_half, gblock(b)))
        ship(d, "wb", part_b)

    for half_rows, n in ((first, 0), (second, 1)):
        arrived(A.at[2, half_rows], f"a2h{n}")
        arrived(A.at[1, half_rows], f"a1h{n}")
    dense(A.at[1], DA.at[1, c])
    dense(A.at[2], DA.at[2, c])
    remote(DA.at[1, c], DA.at[1, c], "asib1", seq=sib)
    remote(DA.at[2, c], DA.at[2, c], "asib2", seq=sib)
    A1, A2 = DA.at[1, c], DA.at[2, c]

    @pl.loop(0, 4)
    def _(b):
        here = cols(b * 256, 256, 256)
        o = (
            acc_o[:, here] + dot(A1[:, here], W[b, 3]) + dot(A2[:, here], W[b, 4])
            + dot(pair[:, 0:256], W[b, 6])
        )
        stage[0, :, :, :, here] = o.astype(BF).reshape(GROUPS, 3, 2, 256)

    gather(0, out_tok, "out")

    arrived(DA.at[1, sib], "asib1")
    arrived(DA.at[2, sib], "asib2")
    for d in (2, 1, 3, 0):
        b = ypeer(d)
        g = gblock(b)
        keep(d, 3, t_dot(half(1, b), g))
        keep(d, 4, t_dot(half(2, b), g))
        ship(d, "wc", part_c)

    arrived(stage.at[1], "gact")

    @pl.loop(0, GROUPS, unroll=4)
    def _(q):
        here = cols(q * 1024, 1024, 1024)
        slope = jax.vjp(gelu_tanh, pre[:, here].astype(F32))[1]
        gp_ref[:, here] = slope(gact_tok[q].reshape(6, 1024).astype(F32))[0].astype(BF)

    def total_of(k):
        far_sum = wg_recv[0, k].astype(F32) + wg_recv[1, k].astype(F32)
        return wg_own[k] + far_sum + wg_recv[2, k].astype(F32)

    for name, rows in (("wa", part_a), ("wb", part_b), ("wc", part_c)):
        for d in range(1, 4):
            arrived(wg_recv.at[d - 1, rows], f"{name}{d}")
    for k in range(5):
        gb_ref[k] = total_of(k)
    gu_ref[...] = total_of(5).T
    gv_ref[...] = total_of(6)
    arrived(stage.at[0], "out")

    @pl.loop(0, GROUPS, unroll=4)
    def _(q):
        out_ref[:, cols(q * 1024, 1024, 1024)] = out_tok[q].reshape(6, 1024)

    most = pl.ds(0, GROUPS - 1)
    top = pl.ds(0, 128)
    sent(G.at[0, most], "g")
    sent(A.at[0, most], "a")
    sent(W.at[0, 7, top], "zfar3")
    sent(W.at[0, 8, top], "zfar4")
    sent(W.at[0, far, top], "farsib")
    for d in range(1, 4):
        sent(W.at[0, low, top], f"low{d}")
        sent(W.at[0, low, top], f"lows{d}")
        sent(W.at[0, fly, top], f"fly{d}")
        sent(W.at[0, fly, top], f"flys{d}")
        sent(W.at[0, far, top], f"far{d}")
        sent(W.at[0, far, top], f"fars{d}")
        sent(latx, f"latx{d}")
        sent(latx, f"bcx{d}")
        sent(wg_send.at[d - 1, part_a], f"wa{d}")
        sent(wg_send.at[d - 1, part_b], f"wb{d}")
        sent(wg_send.at[d - 1, part_c], f"wc{d}")
    sent(G.at[0], "g1")
    sent(G.at[0], "g2")
    for ch in ("gsib", "asib0", "asib1", "asib2"):
        sent(DG.at[0], ch)
    for ch in ("a1h0", "a1h1", "a2h0", "a2h1"):
        sent(A.at[0, first], ch)
    sent(latx.at[pl.ds(0, 7)], "latz")
    sent(latx.at[pl.ds(0, 7)], "bcz")
    sent(lat_all.at[0], "latsib")
    sent(stage.at[0, most], "out")
    sent(stage.at[1, most], "gact")


def exchange(pre_act, grad_out, bfly, low_u, low_v):
    tok = (GROUPS, 3, 2, 1024)
    any_space = pl.BlockSpec(memory_space=pl.ANY)
    vmem = pl.BlockSpec(memory_space=pltpu.VMEM)
    return pl.pallas_call(
        kernel,
        out_shape=(
            jax.ShapeDtypeStruct((6, 32768), BF),
            jax.ShapeDtypeStruct((6, 32768), BF),
            jax.ShapeDtypeStruct((5, 128, 256), F32),
            jax.ShapeDtypeStruct((256, 128), F32),
            jax.ShapeDtypeStruct((128, 256), F32),
        ),
        in_specs=[any_space] * 5,
        out_specs=(vmem,) * 5,
        scratch_shapes=[
            pltpu.VMEM((6, 32768), BF),
            pltpu.VMEM((6, 32768), BF),
            pltpu.VMEM(tok, BF),
            pltpu.VMEM(tok, BF),
            pltpu.VMEM(tok, BF),
            pltpu.VMEM(tok, BF),
            pltpu.VMEM((7, 128, 256), F32),
            pltpu.VMEM((3,) + tok, BF),
            pltpu.VMEM((3,) + tok, BF),
            pltpu.VMEM((3, 2, 192, 1024), BF),
            pltpu.VMEM((2, 192, 1024), BF),
            pltpu.VMEM((192, 1024), BF),
            pltpu.VMEM((192, 1024), BF),
            pltpu.VMEM((4, 9, 256, 256), BF),
            pltpu.VMEM((192, 1024), F32),
            pltpu.VMEM((192, 1024), F32),
            pltpu.VMEM((2,) + tok, BF),
            pltpu.VMEM((GROUPS, 3, 2, 512), BF),
            pltpu.VMEM((3, 8, 3, 2, 512), BF),
            pltpu.VMEM((8, 3, 2, 512), BF),
            pltpu.VMEM((8, 3, 2, 512), BF),
            pltpu.VMEM((3, 2, 512), BF),
            pltpu.VMEM((2, GROUPS, 3, 2, 512), BF),
            pltpu.VMEM((3, 7, 128, 256), BF),
            pltpu.VMEM((3, 7, 128, 256), BF),
            pltpu.SemaphoreType.DMA((len(CHANNELS),)),
            pltpu.SemaphoreType.DMA((len(CHANNELS),)),
        ],
        compiler_params=pltpu.CompilerParams(
            collective_id=0, has_side_effects=True, vmem_limit_bytes=48 * 2**20
        ),
    )(*(pltpu.with_memory_space_constraint(v, pltpu.HBM) for v in (pre_act, grad_out, bfly, low_u, low_v)))


def store_kernel(*refs):
    sources, targets, sem = refs[0:5], refs[5:10], refs[10]
    copies = [
        pltpu.make_async_copy(source, target, sem.at[i])
        for i, (source, target) in enumerate(zip(sources, targets))
    ]
    for copy in copies:
        copy.start()
    for copy in copies:
        copy.wait()


def store(*values):
    any_space = pl.BlockSpec(memory_space=pl.ANY)
    return pl.pallas_call(
        store_kernel,
        out_shape=tuple(jax.ShapeDtypeStruct(v.shape, v.dtype) for v in values),
        in_specs=[pl.BlockSpec(memory_space=pltpu.VMEM)] * 5,
        out_specs=(any_space,) * 5,
        scratch_shapes=[pltpu.SemaphoreType.DMA((5,))],
    )(*values)


def on_device(pre_act, butterfly, low_u, low_v, grad_out):
    parts = exchange(pre_act, grad_out, butterfly[0], low_u, low_v)
    out, grad_pre, gb, gu, gv = parts
    return out, grad_pre, gb[None], gu, gv


def solution(mesh):
    whole = Mesh(mesh.devices.reshape(4, 8, 4, 2), ("x", "z", "y", "seq"))
    hid = ("x", "z", "y")
    tokens = P(hid + ("seq",), None)
    return jax.shard_map(
        on_device,
        mesh=whole,
        in_specs=(tokens, P(hid, None, None, None), P(hid, None), P(None, hid), tokens),
        out_specs=(tokens, tokens, P(hid, None, "seq", None), P(hid, "seq"), P("seq", hid)),
        check_vma=False,
    )
```
